32 devices in a mesh: gx: 4 (over x, core), gy: 4 (over z), gz: 2 (over y).
Axes of the slice: x: 2, y: 2, z: 4, core: 2. Of those that a mesh axis runs over, the one named last changes fastest.
Arguments:
- positions: float32 [3, 512, 128], P(None, ('gx', 'gy', 'gz')), may hold values from -6 to 6
- velocities: float32 [3, 512, 128], P(None, ('gx', 'gy', 'gz')), may hold values from -6 to 6
- weights: float32 [512, 128], P(('gx', 'gy', 'gz')), may hold values from 0.5 to 2
- counts: int32 [512], P(('gx', 'gy', 'gz')), may hold values from 32 to 128
- link_offset: int32 [512, 3], P(('gx', 'gy', 'gz')), may hold values from -16 to 16
- link_mask: int32 [512, 3], P(('gx', 'gy', 'gz')), may hold values 0 or 1
- bin_box: int32 [512, 1], P(('gx', 'gy', 'gz')), may hold values from 0 to 15; in each aligned block of 16 rows (0 to 15, 16 to 31, ...) at most 2 rows name the same one
- bin_cell: int32 [512], P(('gx', 'gy', 'gz')), may hold values from 0 to 4095
- fluid: float32 [3, 16, 32, 256], P(None, 'gx', 'gy', 'gz'), may hold values from -6 to 6
Outputs:
- positions_out: float32 [3, 512, 128], P(None, ('gx', 'gy', 'gz'))
- velocities_out: float32 [3, 512, 128], P(None, ('gx', 'gy', 'gz'))
- fluid_out: float32 [3, 16, 32, 256], P(None, 'gx', 'gy', 'gz')
The draws below stay inside these ranges and needn't reach their ends.
Inputs may be any that keep to these rules, and one draw needn't show every extreme that they name: `bin_box`: the bins of one device name one value at most 2 times; the cell lies in the box at the bin owner's index of gz. `bin_cell`: index of the cell inside its box, first dimension slowest. Slots 0 to counts - 1 of a bin are occupied.
All inputs are finite; a program needn't handle non-finite values. No bound on the sum of `link_mask` on one device may be relied on, other than what follows from the above.
Results may differ from the reference program's by a relative error of at most 0.0001.
Values sent between devices are 32-bit elements; how exact they have to be, the bound alone decides.
No kernel may reach another device: no remote copies, remote signals or barrier semaphores. Data moves between devices by JAX's collectives and lax.ppermute only.
A program may use at most 128 MiB of HBM per device.

```python
import math
import jax
import jax.numpy as jnp
import numpy as np
from jax import lax

S = 128
K_LINKS = 3
SUBSTEPS = 2
BIN_DEV = 16
CX = 4
CY = 8
CZ = 128
NB = 512
BOX_SLOTS = 2
NX = 16
NY = 32
NZ = 256
N_GX = 4
N_GY = 4
N_GZ = 2


def with_ends(drawn, key, low, high):
    extent = drawn.shape
    index_at = [jax.random.randint(jax.random.fold_in(key, axis), (), 0, extent[axis]) for axis in range(len(extent))]
    drawn = drawn.at[tuple(index_at)].set(low)
    longest = extent.index(max(extent))
    index_at[longest] = (index_at[longest] + 1) % extent[longest]
    return drawn.at[tuple(index_at)].set(high)


def block_levels(stream_key, dims, pieces, smallest, high):
    factor_of, own = 1.0, jax.random.fold_in(stream_key, 6)
    for axis_at, parts in pieces:
        heights = jnp.exp(jax.random.uniform(jax.random.fold_in(own, axis_at), (parts,), jnp.float32, smallest / len(pieces), high / len(pieces)))
        factor_of = factor_of * jnp.repeat(heights, dims[axis_at] // parts).reshape([-1 if axis == axis_at else 1 for axis in range(len(dims))])
    return factor_of


def deal_out(stream_key, own, number, rows, amount, top, most, slope):
    order = jax.random.permutation(stream_key, amount)
    heavy_load, ordinary = load_shares(amount, rows * top, most, slope, True), load_shares(amount, rows * top, most, slope, False)
    places = jnp.arange(amount)

    def named(sizes, rotation):
        used = int((sizes > 0).sum())
        fixed = max(1, used // 4)
        shifted = fixed + (places - fixed + rotation * (used - fixed)) % max(1, amount - fixed)
        return jnp.zeros((amount,), jnp.int32).at[order[jnp.where(places < fixed, places, shifted)]].set(jnp.asarray(sizes, jnp.int32))

    sizes = jnp.where(number % 4 == 0, named(heavy_load, number // 4), named(ordinary, number - number // 4 - 1))
    mixed = jax.random.permutation(jax.random.fold_in(own, 3), amount)
    giver, receiver = mixed[0:amount // 2 * 2:2], mixed[1:amount // 2 * 2:2]
    room = jnp.minimum(sizes[giver] - 1, most - sizes[receiver]) // 2
    room = jnp.where((giver == order[0]) | (receiver == order[0]) | (sizes[receiver] == 0), 0, jnp.maximum(room, 0))
    shifted = jax.random.randint(jax.random.fold_in(own, 4), (amount // 2,), 0, 1 << 20) % (room + 1)
    sizes = sizes.at[giver].add(-shifted).at[receiver].add(shifted)
    members = jnp.searchsorted(jnp.cumsum(sizes), jnp.arange(rows * top), side="right").astype(jnp.int32)
    listing = members.reshape(top, rows).T
    listing = listing[jax.random.permutation(jax.random.fold_in(own, 1), rows)]
    rotation = jax.random.randint(jax.random.fold_in(own, 2), (rows, 1), 0, top)
    return jnp.take_along_axis(listing, (jnp.arange(top)[None, :] + rotation) % top, axis=1)


def load_shares(count, total, bound, slope, full):
    loads = [(1 << 20) // math.isqrt(standing ** slope) + 1 for standing in range(1, count + 1)]
    largest = bound if full else min(bound, max(-(-total // count), total * loads[0] // sum(loads)))
    least = 1 if total - largest >= count - 1 else 0
    holding, spare = [largest] + [least] * (count - 1), total - largest - least * (count - 1)
    while spare > 0:
        movable = [i for i in range(1, count) if holding[i] < largest] or [i for i in range(1, count) if holding[i] < bound]
        whole, budget = sum([loads[i] for i in movable]), spare
        for i in movable:
            addition = min(bound - holding[i], max(1, budget * loads[i] // whole), spare)
            holding[i] = holding[i] + addition
            spare = spare - addition
    return np.array(holding)


def bell_draw(stream_key, extent, width, limit, pieces=(), kind=jnp.bfloat16):
    array = width * jax.random.normal(stream_key, extent, jnp.float32)
    if pieces:
        array = array * block_levels(stream_key, extent, pieces, -0.22, 0.18)
    return jnp.clip(array, -limit, limit).astype(kind)


def setup_inputs(seed: int = 0) -> dict:
    seeds = jax.random.split(jax.random.key(seed), 10)
    positions = bell_draw(seeds[0], (3, NB, S), 1.0, 6.0, ((1, 32),), jnp.float32)
    velocities = bell_draw(seeds[1], (3, NB, S), 1.0, 6.0, ((1, 32),), jnp.float32)
    weights = jnp.clip(jnp.exp(math.log(2.0) - 1.3862944 * jax.random.uniform(seeds[2], (NB, S), jnp.float32) ** block_levels(seeds[2], (NB, S), ((0, 32),), -0.2, 0.2)), 0.5, 2.0)
    counts = with_ends(jax.random.randint(seeds[3], (NB,), S // 4, S + 1), jax.random.fold_in(seeds[3], 1), S // 4, S).astype(jnp.int32)
    link_offset = with_ends(jax.random.randint(seeds[4], (NB, K_LINKS), 0 - BIN_DEV, BIN_DEV + 1), jax.random.fold_in(seeds[4], 1), 0 - BIN_DEV, BIN_DEV).astype(jnp.int32)
    link_mask = with_ends((jax.random.randint(seeds[5], (NB, K_LINKS), 0, 4) < 3).astype(jnp.int32), jax.random.fold_in(seeds[5], 1), 0, 1)
    bin_box_keys = jax.random.split(jax.random.fold_in(seeds[6], 1), NB // BIN_DEV)
    bin_box_turns = jax.random.permutation(jax.random.fold_in(seeds[6], 3), NB // BIN_DEV)
    bin_box = jax.vmap(lambda own, number: deal_out(jax.random.fold_in(seeds[6], 2), own, number, BIN_DEV, N_GX * N_GY, 1, BOX_SLOTS, 1))(bin_box_keys, bin_box_turns).reshape((NB, 1))
    bin_cell = with_ends(jax.random.randint(seeds[7], (NB,), 0, CX * CY * CZ), jax.random.fold_in(seeds[7], 1), 0, (CX * CY * CZ) - 1).astype(jnp.int32)
    fluid = bell_draw(seeds[8], (3, NX, NY, NZ), 1.0, 6.0, ((1, 4), (2, 4), (3, 2)), jnp.float32)
    return {"positions": positions, "velocities": velocities, "weights": weights, "counts": counts, "link_offset": link_offset, "link_mask": link_mask, "bin_box": bin_box, "bin_cell": bin_cell, "fluid": fluid}


step_sub = 0.1
stiffness = 0.05
damping = 0.05
drag_rate = 1.0
coupling = 0.004
viscosity = 0.12
highest = lax.Precision.HIGHEST


def contact(own_pos, own_vel, near_pos, near_vel, near_weight):
    distance = jnp.zeros(near_weight.shape[:2] + (own_pos.shape[2], near_weight.shape[2]), jnp.float32)
    for component in range(3):
        offset = own_pos[component][:, None, :, None] - near_pos[component][:, :, None, :]
        distance = distance + offset * offset
    kernel = near_weight[:, :, None, :] * jnp.exp(-0.5 * distance)
    weight_sum = jnp.sum(kernel, axis=(1, 3))
    pull_pos = jnp.einsum("bqij,cbqj->cbi", kernel, near_pos, precision=highest)
    pull_vel = jnp.einsum("bqij,cbqj->cbi", kernel, near_vel, precision=highest)
    return stiffness * (own_pos * weight_sum[None] - pull_pos) - damping * (own_vel * weight_sum[None] - pull_vel)


def advance(widened, state_pos, state_vel, carried, occupied, fluid_seen, neighbour, link_weight, block_bins):
    bin_count = state_pos.shape[1]

    def one_block(block_id, running):
        new_pos, new_vel, pulled = running
        first_bin = (block_id * block_bins).astype(jnp.int32)
        own_pos = lax.dynamic_slice_in_dim(state_pos, first_bin, block_bins, 1)
        own_vel = lax.dynamic_slice_in_dim(state_vel, first_bin, block_bins, 1)
        own_weight = lax.dynamic_slice_in_dim(carried, first_bin, block_bins, 0)
        own_occupied = lax.dynamic_slice_in_dim(occupied, first_bin, block_bins, 0)
        own_fluid = lax.dynamic_slice_in_dim(fluid_seen, first_bin, block_bins, 1)
        link_rows = lax.dynamic_slice_in_dim(neighbour, first_bin, block_bins, 0)
        link_block = lax.dynamic_slice_in_dim(link_weight, first_bin, block_bins, 0)
        nearby = widened[:, link_rows]
        near_pos = jnp.concatenate([own_pos[:, :, None], nearby[0:3]], 2)
        near_vel = jnp.concatenate([own_vel[:, :, None], nearby[3:6]], 2)
        near_weight = jnp.concatenate([own_weight[:, None], nearby[6] * link_block[:, :, None]], 1)
        contact_force = contact(own_pos, own_vel, near_pos, near_vel, near_weight)
        drag_force = drag_rate * (own_fluid[:, :, None] - own_vel)
        moved_vel = own_vel + step_sub * own_occupied[None] * (contact_force + drag_force)
        moved_pos = own_pos + step_sub * own_occupied[None] * moved_vel
        pulled_block = jnp.sum(own_weight[None] * drag_force, axis=2)
        new_pos = lax.dynamic_update_slice_in_dim(new_pos, moved_pos, first_bin, 1)
        new_vel = lax.dynamic_update_slice_in_dim(new_vel, moved_vel, first_bin, 1)
        pulled = lax.dynamic_update_slice_in_dim(pulled, pulled_block, first_bin, 1)
        return new_pos, new_vel, pulled

    start_state = (jnp.zeros_like(state_pos), jnp.zeros_like(state_vel), jnp.zeros((3, bin_count), jnp.float32))
    return lax.fori_loop(0, bin_count // block_bins, one_block, start_state)


def cell_coords(bin_box, bin_cell, bin_count):
    owner_dev = jnp.arange(bin_count, dtype=jnp.int32) // BIN_DEV
    height = owner_dev % N_GZ
    target = bin_box[:, 0]
    row_index = (target // N_GY) * CX + bin_cell // (CY * CZ)
    column_index = (target % N_GY) * CY + (bin_cell // CZ) % CY
    depth_index = height * CZ + bin_cell % CZ
    return row_index, column_index, depth_index


def laplace(velocity_field):
    padded = jnp.pad(velocity_field, ((0, 0), (1, 1), (1, 1), (1, 1)))
    centre = padded[:, 1:-1, 1:-1, 1:-1]
    beside_all = padded[:, 2:, 1:-1, 1:-1] + padded[:, :-2, 1:-1, 1:-1]
    beside_all = beside_all + padded[:, 1:-1, 2:, 1:-1] + padded[:, 1:-1, :-2, 1:-1]
    beside_all = beside_all + padded[:, 1:-1, 1:-1, 2:] + padded[:, 1:-1, 1:-1, :-2]
    return beside_all - 6.0 * centre


def reference(positions, velocities, weights, counts, link_offset, link_mask, bin_box, bin_cell, fluid):
    bin_count = positions.shape[1]
    slot_count = positions.shape[2]
    occupied = (jnp.arange(slot_count, dtype=jnp.int32)[None, :] < counts[:, None]).astype(jnp.float32)
    carried = weights * occupied
    row_index, column_index, depth_index = cell_coords(bin_box, bin_cell, bin_count)
    fluid_seen = fluid[:, row_index, column_index, depth_index]
    neighbour = jnp.arange(bin_count, dtype=jnp.int32)[:, None] + link_offset + BIN_DEV
    link_weight = link_mask.astype(jnp.float32)
    block_bins = 64 if bin_count % 64 == 0 else bin_count
    state_pos = positions
    state_vel = velocities
    pulled_total = jnp.zeros((3, bin_count), jnp.float32)
    for substep in range(SUBSTEPS):
        packed = jnp.concatenate([state_pos, state_vel, carried[None]], 0)
        widened = jnp.pad(packed, ((0, 0), (BIN_DEV, BIN_DEV), (0, 0)))
        state_pos, state_vel, pulled = advance(widened, state_pos, state_vel, carried, occupied, fluid_seen, neighbour, link_weight, block_bins)
        pulled_total = pulled_total + pulled
    source = jnp.zeros(fluid.shape, jnp.float32).at[:, row_index, column_index, depth_index].add(-coupling * pulled_total)
    first_rate = viscosity * laplace(fluid) + source
    middle = fluid + first_rate
    second_rate = viscosity * laplace(middle) + source
    fluid_out = fluid + 0.5 * (first_rate + second_rate)
    return state_pos, state_vel, fluid_out
```

```python
import functools
import math

import jax
import jax.numpy as jnp
from jax import lax
from jax.experimental import pallas as pl
from jax.experimental.pallas import tpu as pltpu
from jax.sharding import PartitionSpec as P

step_sub = 0.1
stiffness = 0.05
damping = 0.05
drag_rate = 1.0
coupling = 0.004
viscosity = 0.12
log2e = 1.4426950408889634

AXES = ("gx", "gy", "gz")
F32 = jnp.float32
BF16 = jnp.bfloat16
VMEM = pl.BlockSpec(memory_space=pltpu.VMEM)
SMEM = pl.BlockSpec(memory_space=pltpu.SMEM)
LANES = 128


def iota(shape, dim):
    return lax.broadcasted_iota(jnp.int32, shape, dim)


def nt(a, b, precision=None):
    return lax.dot_general(
        a, b, (((1,), (1,)), ((), ())), preferred_element_type=F32, precision=precision
    )


def tn(a, b):
    return lax.dot_general(a, b, (((0,), (0,)), ((), ())), preferred_element_type=F32)


def nn(a, b):
    return jnp.dot(a, b, preferred_element_type=F32)


def pieces_2(value):
    high = value.astype(BF16).astype(F32)
    return high, value - high


def pieces_3(value):
    high = value.astype(BF16).astype(F32)
    rest = value - high
    middle = rest.astype(BF16).astype(F32)
    return high, middle, rest - middle


def call(body, outs, ins, scratch=(), cost=None):
    return pl.pallas_call(
        body,
        out_shape=[jax.ShapeDtypeStruct(shape, F32) for shape in outs],
        in_specs=ins,
        out_specs=[VMEM] * len(outs),
        scratch_shapes=scratch,
        compiler_params=pltpu.CompilerParams(vmem_limit_bytes=24 * 1024 * 1024),
        cost_estimate=cost,
    )


def slot_lane(field, slot, n, bins):
    groups = LANES // n
    per_group = bins // groups
    return (slot // per_group) * (LANES // groups) + field * per_group + slot % per_group


def prep_body(
    n, pos, vel, weights, fluid, counts, box, cell, msg, send, face_low, face_high
):
    bins = pos.shape[1]
    cx, cy, cz = fluid.shape[1:]
    lane = iota((8, LANES), 1)
    row = iota((8, LANES), 0)
    for k in range(bins):
        for c in range(3):
            msg[k, c : c + 1, :] = pos[c, k : k + 1, :]
            msg[k, c + 4 : c + 5, :] = vel[c, k : k + 1, :]
        occupied = iota((1, LANES), 1) < counts[k]
        msg[k, 3:4, :] = jnp.where(occupied, weights[k : k + 1, :], 0.0)
        msg[k, 7:8, :] = jnp.zeros((1, LANES), F32)
    gy_count = lax.axis_size("gy")
    height = lax.axis_index("gz")
    ids = jnp.zeros((8, LANES), F32)
    for k in range(bins):
        target, inside = box[k], cell[k]
        x = lax.div(target, gy_count) * cx + lax.div(inside, cy * cz)
        y = lax.rem(target, gy_count) * cy + lax.rem(lax.div(inside, cz), cy)
        z = height * cz + lax.rem(inside, cz)
        for field, value in enumerate((x, y, z)):
            ids = jnp.where(lane == slot_lane(field, k, n, bins), value.astype(F32), ids)
    pick = jnp.where(
        ((row == 1) & (lane == 0))
        | ((row == 2) & (lane == 1))
        | ((row == 3) & (lane == cz - 2))
        | ((row == 4) & (lane == cz - 1)),
        1.0,
        0.0,
    )
    flat = fluid[...].reshape(3 * cx * cy, cz)
    flat = jnp.concatenate([flat, jnp.zeros((LANES - 3 * cx * cy, cz), F32)], 0)
    faces = nt(pick, flat, lax.Precision.HIGHEST)
    chunk = jnp.where(row == 0, ids, faces)
    for d in range(n):
        send[d] = chunk
    face_low[...] = fluid[:, 0:2]
    face_high[...] = fluid[:, cx - 2 : cx]


def gather_body(n, bins, recv, fluid, out):
    cx, cy, cz = fluid.shape[1:]
    per_group = bins // (LANES // n)
    cells = cx * cy
    ids = recv[:, 0, :]
    x = ids - (lax.axis_index("gx") * cx).astype(F32)
    y = pltpu.roll(ids, LANES - per_group, 1) - (lax.axis_index("gy") * cy).astype(F32)
    z = pltpu.roll(ids, LANES - 2 * per_group, 1) - (lax.axis_index("gz") * cz).astype(F32)
    mine = (x >= 0) & (x < cx) & (y >= 0) & (y < cy) & (z >= 0) & (z < cz)
    column_code = jnp.where(mine, x * cy + y, -1.0).astype(jnp.int32)
    depth_code = jnp.where(mine, z, -1.0).astype(jnp.int32)
    flat = fluid[...].reshape(3 * cells, cz)
    high, low = pieces_2(flat)
    table = jnp.concatenate([high, low, jnp.zeros((256 - 6 * cells, cz), F32)], 0).astype(BF16)
    lane_z = iota((n, cz), 1)
    lane_cell = iota((n, 256), 1) % cells
    one_hot = []
    masks = []
    for k in range(bins):
        at = slot_lane(0, k, n, bins)
        one_hot.append(jnp.where(depth_code[:, at : at + 1] == lane_z, 1.0, 0.0))
        masks.append(column_code[:, at : at + 1] == lane_cell)
    picked = nt(jnp.concatenate(one_hot, 0).astype(BF16), table)
    kept = jnp.where(jnp.concatenate(masks, 0), picked, 0.0).astype(BF16)
    rows = iota((256, LANES), 0)
    fold = jnp.where(
        (rows < 6 * cells) & ((rows // cells) % 3 == iota((256, LANES), 1) % 4), 1.0, 0.0
    ).astype(BF16)
    spread = nn(kept, fold)
    slot_of_lane = iota((n, LANES), 1) // 4
    total = jnp.zeros((n, LANES), F32)
    for k in range(bins):
        total = total + jnp.where(slot_of_lane == k, spread[k * n : (k + 1) * n], 0.0)
    out[...] = total


def load_block(block, row, index, stack, weighted):
    square = block * block
    norm = (-0.5 * log2e) * (
        square[0:1] + square[1:2] + square[2:3]
    )
    near = jnp.where(
        row < 3, block, jnp.where(row == 3, norm, jnp.where(row == 4, 1.0, 0.0))
    )
    high, middle, low = pieces_3(near)
    stack[index] = jnp.concatenate([high, high, middle, middle, high, low], 0).astype(BF16)
    carried = block[3:4]
    product = jnp.where(row == 3, carried, jnp.where(row == 7, 0.0, block * carried))
    high, low = pieces_2(product)
    weighted[index] = jnp.concatenate([high, low], 0).astype(BF16)
    return norm


def own_side(block, norm, row):
    own = jnp.where(
        row < 3, block * log2e, jnp.where(row == 3, 1.0, jnp.where(row == 4, norm, 0.0))
    )
    high, middle, low = pieces_3(own)
    return jnp.concatenate([high, middle, high, middle, low, high], 0).astype(BF16)


def pair_sums(k, d, n, bins, own, stack, weighted, offset, mask):
    near = [bins + k]
    heavy = [bins + k]
    for q in range(offset.shape[0]):
        shift = offset[q, k]
        near.append(bins + k + shift)
        whole = d * bins + k + shift
        linked = (mask[q, k] != 0) & (whole >= 0) & (whole < n * bins)
        heavy.append(jnp.where(linked, bins + k + shift, 3 * bins))
    others = jnp.concatenate([stack[index] for index in near], 1)
    masses = jnp.concatenate([weighted[index] for index in heavy], 1)
    kernel = jnp.exp2(tn(own, others))
    high = kernel.astype(BF16)
    low = (kernel - high.astype(F32)).astype(BF16)
    first = nt(masses, high)
    second = nt(masses, low)
    return first[0:8] + first[8:16] + second[0:8]


def contact_force(block, sums):
    gap = block * sums[3:4] - sums
    return stiffness * pltpu.roll(gap, 4, 0) - damping * gap


def flat_id():
    return (
        lax.axis_index("gx") * lax.axis_size("gy") + lax.axis_index("gy")
    ) * lax.axis_size("gz") + lax.axis_index("gz")


def first_body(
    n, own, before, after, seen, counts, offset, mask, moved, send, stack, weighted, norms
):
    bins = own.shape[0]
    d = flat_id()
    row = iota((8, LANES), 0)
    lane = iota((8, LANES), 1)
    for k in range(bins):
        load_block(before[k], row, k, stack, weighted)
        norms[k : k + 1, :] = load_block(own[k], row, bins + k, stack, weighted)
        load_block(after[k], row, 2 * bins + k, stack, weighted)
    weighted[3 * bins] = jnp.zeros((16, LANES), BF16)
    groups = LANES // n
    per_group = bins // groups
    field = jnp.where(row >= 4, row - 4, 3)
    deposit = jnp.zeros((8, LANES), F32)
    for k in range(bins):
        block = own[k]
        sums = pair_sums(
            k, d, n, bins, own_side(block, norms[k : k + 1, :], row), stack, weighted, offset, mask
        )
        force = contact_force(block, sums)
        occupied = jnp.where(lane < counts[k], step_sub, 0.0)
        new_vel = block + occupied * (force - drag_rate * block)
        new_pos = block + occupied * pltpu.roll(new_vel, 4, 0)
        result = jnp.where(row < 3, new_pos, jnp.where(row == 3, block, new_vel))
        moved[k] = result
        load = jnp.where(row == 3, block, block[3:4] * (block + new_vel))
        column = jnp.sum(load, axis=1, keepdims=True)
        base = slot_lane(0, k, n, bins)
        place = (lane == base + per_group * field) & (row >= 3) & (row < 7)
        deposit = deposit + jnp.where(place, column, 0.0)
    deposit = jnp.sum(deposit, axis=0, keepdims=True)
    send[...] = jnp.broadcast_to(
        jnp.where(row == 3, deposit, 0.0)[None], (n, 8, LANES)
    )
    values = seen[...]
    send[:, 0, :] = pltpu.roll(values, 1, 0)
    send[:, 1, :] = values
    send[:, 2, :] = pltpu.roll(values, n - 1, 0)


def second_body(
    n, own, before, after, recv, counts, offset, mask, pos, vel, stack, weighted, state
):
    bins = own.shape[0]
    d = flat_id()
    row = iota((8, LANES), 0)
    lane = iota((8, LANES), 1)
    seen = recv[0]
    for s in range(1, n):
        seen = seen + recv[s]
    columns = [
        jnp.transpose(jnp.broadcast_to(seen[part : part + 1], (LANES, LANES)))
        for part in range(3)
    ]
    rate = jnp.where(row < 4, step_sub * step_sub, step_sub) * drag_rate

    def push(part, k):
        pair = columns[part][8 * (k // 2) : 8 * (k // 2) + 8]
        other = pltpu.roll(pair, 4, 0)
        here = (row < 4) if k % 2 == 0 else (row >= 4)
        both = jnp.where(here, pair, other)
        return jnp.where((row == 3) | (row == 7), 0.0, both * rate), both

    for k in range(bins):
        load_block(before[k] + push(0, k)[0], row, k, stack, weighted)
        load_block(after[k] + push(2, k)[0], row, 2 * bins + k, stack, weighted)
        block = own[k] + jnp.where(lane < counts[k], push(1, k)[0], 0.0)
        state[k] = block
        load_block(block, row, bins + k, stack, weighted)
    weighted[3 * bins] = jnp.zeros((16, LANES), BF16)
    for k in range(bins):
        block = state[k]
        square = block * block
        norm = (-0.5 * log2e) * (square[0:1] + square[1:2] + square[2:3])
        sums = pair_sums(
            k, d, n, bins, own_side(block, norm, row), stack, weighted, offset, mask
        )
        force = contact_force(block, sums)
        occupied = jnp.where(lane < counts[k], step_sub, 0.0)
        fluid_seen = push(1, k)[1]
        new_vel = block + occupied * (force + drag_rate * (fluid_seen - block))
        new_pos = block + occupied * pltpu.roll(new_vel, 4, 0)
        for c in range(3):
            pos[c, k : k + 1, :] = new_pos[c : c + 1]
            vel[c, k : k + 1, :] = new_vel[c + 4 : c + 5]


def side_body(fluid, from_low, from_high, low, high):
    cx, cy = fluid.shape[1:3]
    gx = lax.axis_index("gx")
    has_low = jnp.where(gx > 0, 1.0, 0.0)
    has_high = jnp.where(gx < lax.axis_size("gx") - 1, 1.0, 0.0)
    for j in range(2):
        for c in range(3):
            for i in range(cx + 2):
                at = (j * 3 + c) * (cx + 2) + i
                for out, y in ((low, j), (high, cy - 2 + j)):
                    if i == 0:
                        line = from_low[c, 1, y : y + 1, :] * has_low
                    elif i == cx + 1:
                        line = from_high[c, 0, y : y + 1, :] * has_high
                    else:
                        line = fluid[c, i - 1, y : y + 1, :]
                    out[at : at + 1, :] = line
    used = 6 * (cx + 2)
    if used < low.shape[0]:
        low[used:, :] = jnp.zeros((low.shape[0] - used, LANES), F32)
        high[used:, :] = jnp.zeros((low.shape[0] - used, LANES), F32)


def laplace(at, x):
    centre = at(x)
    tall, wide = centre.shape
    total = at(x + 1) + at(x - 1)
    total = total + pltpu.roll(centre, 1, 0) + pltpu.roll(centre, tall - 1, 0)
    total = total + pltpu.roll(centre, 1, 1) + pltpu.roll(centre, wide - 1, 1)
    return viscosity * (total - 6.0 * centre)


def stencil_body(
    n, fluid, x_low, x_high, y_low, y_high, recv, around, part, faces, rates
):
    cx, cy, cz = fluid.shape[1:]
    gx, gy, gz = (lax.axis_index(a) for a in AXES)
    nx, ny, nz = (lax.axis_size(a) for a in AXES)
    tall, wide = 2 * cy, 2 * cz
    deep = cx + 4

    def exists(dx, dy, dz):
        ok = (gx + dx >= 0) & (gx + dx < nx) & (gy + dy >= 0) & (gy + dy < ny)
        return ok & (gz + dz >= 0) & (gz + dz < nz)

    def chunk(dx, dy, dz):
        source = ((gx + dx) * ny + gy + dy) * nz + gz + dz
        value = recv[jnp.clip(source, 0, n - 1)]
        return jnp.where(exists(dx, dy, dz), value, 0.0)

    def columns(dx, dy):
        above, below = chunk(dx, dy, 1), chunk(dx, dy, -1)
        faces[...] = jnp.zeros((LANES, LANES), F32)
        faces[0:2, :] = above[1:3]
        faces[cz - 2 : cz, :] = below[3:5]
        return jnp.transpose(faces[...])

    own_z = columns(0, 0)
    low_z, high_z = columns(-1, 0), columns(1, 0)
    left_z, right_z = columns(0, -1), columns(0, 1)
    x_on = [jnp.where(exists(-1, 0, 0), 1.0, 0.0), jnp.where(exists(1, 0, 0), 1.0, 0.0)]
    y_on = [jnp.where(exists(0, -1, 0), 1.0, 0.0), jnp.where(exists(0, 1, 0), 1.0, 0.0)]
    row = iota((cy, cz), 0)

    def y_line(ref, j, c, i):
        at = (j * 3 + c) * (cx + 2) + i
        return ref[at : at + 1, :]

    for c in range(3):
        for x in range(-2, cx + 2):
            if x < 0:
                core = x_low[c, x + 2] * x_on[0]
            elif x >= cx:
                core = x_high[c, x - cx] * x_on[1]
            else:
                core = fluid[c, x]
            beyond = jnp.zeros((cy, cz), F32)
            if 0 <= x < cx:
                at = (c * cx + x) * cy
                beyond = own_z[at : at + cy]
            elif x == -1:
                at = (c * cx + cx - 1) * cy
                beyond = low_z[at : at + cy]
            elif x == cx:
                at = c * cx * cy
                beyond = high_z[at : at + cy]
            around[c, x % deep, 0:cy, 0:cz] = core
            around[c, x % deep, 0:cy, cz:wide] = beyond
            side = jnp.zeros((cy, cz), F32)
            side_z = jnp.zeros((cy, cz), F32)
            if -1 <= x <= cx:
                side = jnp.where(row == 0, y_line(y_high, 0, c, x + 1) * y_on[1], side)
                side = jnp.where(row == 1, y_line(y_high, 1, c, x + 1) * y_on[1], side)
                side = jnp.where(row == cy - 2, y_line(y_low, 0, c, x + 1) * y_on[0], side)
                side = jnp.where(row == cy - 1, y_line(y_low, 1, c, x + 1) * y_on[0], side)
            if 0 <= x < cx:
                at = (c * cx + x) * cy
                side_z = jnp.where(row == 0, right_z[at : at + 1], side_z)
                side_z = jnp.where(row == cy - 1, left_z[at + cy - 1 : at + cy], side_z)
            around[c, x % deep, cy:tall, 0:cz] = side
            around[c, x % deep, cy:tall, cz:wide] = side_z

    y_row, z_lane = iota((tall, wide), 0), iota((tall, wide), 1)
    inside = jnp.where(y_row < cy, 1.0, 0.0)
    inside = jnp.where(y_row == cy, y_on[1], jnp.where(y_row == tall - 1, y_on[0], inside))
    deep_on = jnp.where(z_lane < cz, 1.0, 0.0)
    deep_on = jnp.where(z_lane == cz, jnp.where(exists(0, 0, 1), 1.0, 0.0), deep_on)
    deep_on = jnp.where(z_lane == wide - 1, jnp.where(exists(0, 0, -1), 1.0, 0.0), deep_on)
    inside = inside * deep_on
    for c in range(3):
        for x in range(-1, cx + 1):
            rate = laplace(lambda i: around[c, i % deep], x) * inside
            if x < 0:
                rate = rate * x_on[0]
            elif x == cx:
                rate = rate * x_on[1]
            rates[c, x + 1] = rate
        for x in range(cx):
            again = laplace(lambda i: rates[c, i + 1], x)
            total = around[c, x] + rates[c, x + 1] + 0.5 * again
            part[c, x] = total[0:cy, 0:cz]


def deposit_body(n, bins, part, around, ids, recv, out, table, low_table, depth, field):
    cx, cy, cz = part.shape[1:]
    deep = cx + 4
    tall, wide = 2 * cy, 2 * cz
    groups = LANES // n
    per_group = bins // groups
    planes = (cx + 2) * tall

    def packed(ref, which):
        turned = jnp.transpose(
            jnp.concatenate(
                [ref[:, which, :]] + ([jnp.zeros((LANES - n, LANES), F32)] if n < LANES else []), 0
            )
        )
        span = LANES // groups
        total = turned[0:span]
        for g in range(1, groups):
            total = total + pltpu.roll(turned[g * span : (g + 1) * span], g * n, 1)
        return total

    where = packed(ids, 0)
    loads = packed(recv, 3)
    x = where[0:per_group] - (lax.axis_index("gx") * cx - 1).astype(F32)
    y = where[per_group : 2 * per_group] - (lax.axis_index("gy") * cy).astype(F32)
    z = where[2 * per_group : 3 * per_group] - (lax.axis_index("gz") * cz).astype(F32)
    near = (x >= 0) & (x < cx + 2) & (y >= -1) & (y <= cy) & (z >= -1) & (z <= cz)
    y = jnp.where(y < 0, y + tall, y)
    z = jnp.where(z < 0, z + wide, z)
    plane_code = jnp.where(near, x * tall + y, -1.0).astype(jnp.int32)
    depth_code = jnp.where(near, z, -1.0).astype(jnp.int32)
    plane_row = iota((planes, LANES), 0)
    depth_row = iota((wide, LANES), 0)
    for r in range(per_group):
        at = r * LANES
        hit = plane_code[r : r + 1] == plane_row
        for f in range(4):
            load = loads[f * per_group + r : f * per_group + r + 1]
            high, low = pieces_2(load)
            table[f * planes : (f + 1) * planes, at : at + LANES] = jnp.where(
                hit, high, 0.0
            ).astype(BF16)
            low_table[f * planes : (f + 1) * planes, at : at + LANES] = jnp.where(
                hit, low, 0.0
            ).astype(BF16)
        depth[:, at : at + LANES] = jnp.where(
            depth_code[r : r + 1] == depth_row, 1.0, 0.0
        ).astype(BF16)
    spread = nt(table[...], depth[...]) + nt(low_table[...], depth[...])
    factor = coupling * drag_rate * (2.0 - step_sub * drag_rate)
    for c in range(3):
        for i in range(cx + 2):
            moment = spread[c * planes + i * tall : c * planes + (i + 1) * tall]
            mass = spread[3 * planes + i * tall : 3 * planes + (i + 1) * tall]
            field[c, i] = (coupling * drag_rate) * moment - factor * around[
                c, (i - 1) % deep
            ] * mass
        for x in range(cx):
            rate = laplace(lambda i: field[c, i + 1], x)
            total = field[c, x + 1] + 0.5 * rate
            out[c, x] = part[c, x] + total[0:cy, 0:cz]


def ring(n, step):
    return [(i, (i + step) % n) for i in range(n)]


def local(positions, velocities, weights, counts, link_offset, link_mask, bin_box, bin_cell, fluid):
    n = lax.axis_size(AXES)
    nx, ny = lax.axis_size("gx"), lax.axis_size("gy")
    bins = positions.shape[1]
    cx, cy, cz = fluid.shape[1:]
    offset, mask = link_offset.T, link_mask.T
    side_rows = -(-6 * (cx + 2) // 8) * 8

    own, send, face_low, face_high = call(
        functools.partial(prep_body, n),
        [(bins, 8, LANES), (n, 8, LANES), (3, 2, cy, cz), (3, 2, cy, cz)],
        [VMEM] * 4 + [SMEM] * 3,
    )(positions, velocities, weights, fluid, counts, bin_box[:, 0], bin_cell)
    ids = lax.all_to_all(send, AXES, 0, 0, tiled=True)
    before = lax.ppermute(own, AXES, ring(n, 1))
    after = lax.ppermute(own, AXES, ring(n, -1))
    x_low = lax.ppermute(face_high, "gx", ring(nx, 1))
    x_high = lax.ppermute(face_low, "gx", ring(nx, -1))

    (seen,) = call(functools.partial(gather_body, n, bins), [(n, LANES)], [VMEM] * 2)(ids, fluid)
    pair_scratch = [
        pltpu.VMEM((3 * bins + 1, 48, LANES), BF16),
        pltpu.VMEM((3 * bins + 1, 16, LANES), BF16),
    ]
    moved, send = call(
        functools.partial(first_body, n),
        [(bins, 8, LANES), (n, 8, LANES)],
        [VMEM] * 4 + [SMEM] * 3,
        pair_scratch + [pltpu.VMEM((bins, LANES), F32)],
    )(own, before, after, seen, counts, offset, mask)
    replies = lax.all_to_all(send, AXES, 0, 0, tiled=True)
    before = lax.ppermute(moved, AXES, ring(n, 1))
    after = lax.ppermute(moved, AXES, ring(n, -1))

    side_low, side_high = call(side_body, [(side_rows, LANES)] * 2, [VMEM] * 3)(
        fluid, x_low, x_high
    )
    y_low = lax.ppermute(side_high, "gy", ring(ny, 1))
    y_high = lax.ppermute(side_low, "gy", ring(ny, -1))
    around, part = call(
        functools.partial(stencil_body, n),
        [(3, cx + 4, 2 * cy, 2 * cz), (3, cx, cy, cz)],
        [VMEM] * 6,
        [pltpu.VMEM((LANES, LANES), F32), pltpu.VMEM((3, cx + 2, 2 * cy, 2 * cz), F32)],
    )(fluid, x_low, x_high, y_low, y_high, ids)
    positions_out, velocities_out = call(
        functools.partial(second_body, n),
        [positions.shape, velocities.shape],
        [VMEM] * 4 + [SMEM] * 3,
        pair_scratch + [pltpu.VMEM((bins, 8, LANES), F32)],
    )(moved, before, after, replies, counts, offset, mask)
    lanes = bins * n
    planes = (cx + 2) * 2 * cy
    (fluid_out,) = call(
        functools.partial(deposit_body, n, bins),
        [fluid.shape],
        [VMEM] * 4,
        [
            pltpu.VMEM((4 * planes, lanes), BF16),
            pltpu.VMEM((4 * planes, lanes), BF16),
            pltpu.VMEM((2 * cz, lanes), BF16),
            pltpu.VMEM((3, cx + 2, 2 * cy, 2 * cz), F32),
        ],
    )(part, around, ids, replies)
    return positions_out, velocities_out, fluid_out


def solution(mesh):
    in_specs = (
        P(None, AXES, None),
        P(None, AXES, None),
        P(AXES, None),
        P(AXES),
        P(AXES, None),
        P(AXES, None),
        P(AXES, None),
        P(AXES),
        P(None, "gx", "gy", "gz"),
    )
    out_specs = (
        P(None, AXES, None),
        P(None, AXES, None),
        P(None, "gx", "gy", "gz"),
    )
    return jax.shard_map(local, mesh=mesh, in_specs=in_specs, out_specs=out_specs, check_vma=False)
```

```python
import functools

import jax
import jax.numpy as jnp
from jax import lax
from jax.experimental import pallas as pl
from jax.experimental.pallas import tpu as pltpu
from jax.sharding import PartitionSpec as P


step_sub = 0.1
stiffness = 0.05
damping = 0.05
drag_rate = 1.0
coupling = 0.004
viscosity = 0.12
log2e = 1.4426950408889634

AXES = ("gx", "gy", "gz")
F32 = jnp.float32
BF16 = jnp.bfloat16
VMEM = pl.BlockSpec(memory_space=pltpu.VMEM)
ANY = pl.BlockSpec(memory_space=pl.ANY)
HBM = pl.BlockSpec(memory_space=pltpu.HBM)
LANES = 128


def iota(shape, dim):
    return lax.broadcasted_iota(jnp.int32, shape, dim)


def nt(a, b, precision=None):
    return lax.dot_general(
        a, b, (((1,), (1,)), ((), ())), preferred_element_type=F32, precision=precision
    )


def tn(a, b):
    return lax.dot_general(a, b, (((0,), (0,)), ((), ())), preferred_element_type=F32)


def nn(a, b):
    return jnp.dot(a, b, preferred_element_type=F32)


def pieces_2(value):
    high = value.astype(BF16).astype(F32)
    return high, value - high


def pieces_3(value):
    high = value.astype(BF16).astype(F32)
    rest = value - high
    middle = rest.astype(BF16).astype(F32)
    return high, middle, rest - middle


def call(body, outs, ins, scratch=(), cost=None):
    return pl.pallas_call(
        body,
        out_shape=[jax.ShapeDtypeStruct(shape, F32) for shape in outs],
        in_specs=ins,
        out_specs=[VMEM] * len(outs),
        scratch_shapes=scratch,
        compiler_params=pltpu.CompilerParams(vmem_limit_bytes=24 * 1024 * 1024),
        cost_estimate=cost,
    )


def slot_lane(field, slot, n, bins):
    groups = LANES // n
    per_group = bins // groups
    return (slot // per_group) * (LANES // groups) + field * per_group + slot % per_group


def fetch(sources, targets, sems):
    copies = [
        pltpu.make_async_copy(source, target, sems.at[i])
        for i, (source, target) in enumerate(zip(sources, targets))
    ]
    for copy in copies:
        copy.start()
    return copies


def prep_body(n, *refs):
    sources, (msg, send, face_low, face_high), locals_, sems = (
        refs[:7],
        refs[7:11],
        refs[11:18],
        refs[18],
    )
    copies = fetch(sources, locals_, sems)
    pos, vel, weights, fluid, counts, box, cell = locals_
    for copy in copies:
        copy.wait()
    bins = pos.shape[1]
    cx, cy, cz = fluid.shape[1:]
    lane = iota((8, LANES), 1)
    row = iota((8, LANES), 0)
    for k in range(bins):
        for c in range(3):
            msg[k, c : c + 1, :] = pos[c, k : k + 1, :]
            msg[k, c + 4 : c + 5, :] = vel[c, k : k + 1, :]
        occupied = iota((1, LANES), 1) < counts[k]
        msg[k, 3:4, :] = jnp.where(occupied, weights[k : k + 1, :], 0.0)
        msg[k, 7:8, :] = jnp.zeros((1, LANES), F32)
    gy_count = lax.axis_size("gy")
    height = lax.axis_index("gz")
    ids = jnp.zeros((8, LANES), F32)
    for k in range(bins):
        target, inside = box[k], cell[k]
        x = lax.div(target, gy_count) * cx + lax.div(inside, cy * cz)
        y = lax.rem(target, gy_count) * cy + lax.rem(lax.div(inside, cz), cy)
        z = height * cz + lax.rem(inside, cz)
        for field, value in enumerate((x, y, z)):
            ids = jnp.where(lane == slot_lane(field, k, n, bins), value.astype(F32), ids)
    pick = jnp.where(
        ((row == 1) & (lane == 0))
        | ((row == 2) & (lane == 1))
        | ((row == 3) & (lane == cz - 2))
        | ((row == 4) & (lane == cz - 1)),
        1.0,
        0.0,
    )
    flat = fluid[...].reshape(3 * cx * cy, cz)
    flat = jnp.concatenate([flat, jnp.zeros((LANES - 3 * cx * cy, cz), F32)], 0)
    faces = nt(pick, flat, lax.Precision.HIGHEST)
    chunk = jnp.where(row == 0, ids, faces)
    for d in range(n):
        send[d] = chunk
    face_low[...] = fluid[:, 0:2]
    face_high[...] = fluid[:, cx - 2 : cx]


def gather_body(n, bins, recv, fluid, deposit, send):
    cx, cy, cz = fluid.shape[1:]
    per_group = bins // (LANES // n)
    cells = cx * cy
    ids = recv[:, 0, :]
    x = ids - (lax.axis_index("gx") * cx).astype(F32)
    y = pltpu.roll(ids, LANES - per_group, 1) - (lax.axis_index("gy") * cy).astype(F32)
    z = pltpu.roll(ids, LANES - 2 * per_group, 1) - (lax.axis_index("gz") * cz).astype(F32)
    mine = (x >= 0) & (x < cx) & (y >= 0) & (y < cy) & (z >= 0) & (z < cz)
    column_code = jnp.where(mine, x * cy + y, -1.0).astype(jnp.int32)
    depth_code = jnp.where(mine, z, -1.0).astype(jnp.int32)
    flat = fluid[...].reshape(3 * cells, cz)
    high, low = pieces_2(flat)
    table = jnp.concatenate([high, low, jnp.zeros((256 - 6 * cells, cz), F32)], 0).astype(BF16)
    lane_z = iota((n, cz), 1)
    lane_cell = iota((n, 256), 1) % cells
    one_hot = []
    masks = []
    for k in range(bins):
        at = slot_lane(0, k, n, bins)
        one_hot.append(jnp.where(depth_code[:, at : at + 1] == lane_z, 1.0, 0.0))
        masks.append(column_code[:, at : at + 1] == lane_cell)
    picked = nt(jnp.concatenate(one_hot, 0).astype(BF16), table)
    kept = jnp.where(jnp.concatenate(masks, 0), picked, 0.0).astype(BF16)
    rows = iota((256, LANES), 0)
    fold = jnp.where(
        (rows < 6 * cells) & ((rows // cells) % 3 == iota((256, LANES), 1) % 4), 1.0, 0.0
    ).astype(BF16)
    spread = nn(kept, fold)
    slot_of_lane = iota((n, LANES), 1) // 4
    total = jnp.zeros((n, LANES), F32)
    for k in range(bins):
        total = total + jnp.where(slot_of_lane == k, spread[k * n : (k + 1) * n], 0.0)
    send[:, 0, :] = pltpu.roll(total, 1, 0)
    send[:, 1, :] = total
    send[:, 2, :] = pltpu.roll(total, n - 1, 0)
    send[:, 3, :] = jnp.broadcast_to(deposit[0:1], (n, LANES))


def load_block(block, row, index, stack, weighted):
    square = block * block
    norm = (-0.5 * log2e) * (
        square[0:1] + square[1:2] + square[2:3]
    )
    near = jnp.where(
        row < 3, block, jnp.where(row == 3, norm, jnp.where(row == 4, 1.0, 0.0))
    )
    high, middle, low = pieces_3(near)
    stack[index] = jnp.concatenate([high, high, middle, middle, high, low], 0).astype(BF16)
    carried = block[3:4]
    product = jnp.where(row == 3, carried, jnp.where(row == 7, 0.0, block * carried))
    high, low = pieces_2(product)
    weighted[index] = jnp.concatenate([high, low], 0).astype(BF16)
    return norm


def own_side(block, norm, row):
    own = jnp.where(
        row < 3, block * log2e, jnp.where(row == 3, 1.0, jnp.where(row == 4, norm, 0.0))
    )
    high, middle, low = pieces_3(own)
    return jnp.concatenate([high, middle, high, middle, low, high], 0).astype(BF16)


def pair_sums(d, n, bins, own_of, stack, weighted, offset, mask):
    def exponents(k):
        near = [bins + k]
        heavy = [bins + k]
        for q in range(offset.shape[0]):
            shift = offset[q, k]
            near.append(bins + k + shift)
            whole = d * bins + k + shift
            linked = (mask[q, k] != 0) & (whole >= 0) & (whole < n * bins)
            heavy.append(jnp.where(linked, bins + k + shift, 3 * bins))
        others = jnp.concatenate([stack[index] for index in near], 1)
        masses = jnp.concatenate([weighted[index] for index in heavy], 1)
        return tn(own_of(k), others), masses

    sums = []
    following = exponents(0)
    for k in range(bins):
        value, masses = following
        if k + 1 < bins:
            following = exponents(k + 1)
        kernel = jnp.exp2(value)
        high = kernel.astype(BF16)
        low = (kernel - high.astype(F32)).astype(BF16)
        turned = jnp.transpose(nt(high, masses) + nt(low, masses))
        sums.append(turned[0:8] + turned[8:16])
    return sums


def contact_force(block, sums):
    gap = block * sums[3:4] - sums
    return stiffness * pltpu.roll(gap, 4, 0) - damping * gap


def flat_id():
    return (
        lax.axis_index("gx") * lax.axis_size("gy") + lax.axis_index("gy")
    ) * lax.axis_size("gz") + lax.axis_index("gz")


def first_body(
    n, own, before, after, *refs
):
    copies = fetch(refs[0:3], refs[8:11], refs[11])
    moved, deposit, stack, weighted, norms, counts, offset, mask = refs[3:11]
    bins = own.shape[0]
    d = flat_id()
    row = iota((8, LANES), 0)
    lane = iota((8, LANES), 1)
    for k in range(bins):
        load_block(before[k], row, k, stack, weighted)
        norms[k : k + 1, :] = load_block(own[k], row, bins + k, stack, weighted)
        load_block(after[k], row, 2 * bins + k, stack, weighted)
    weighted[3 * bins] = jnp.zeros((16, LANES), BF16)
    for copy in copies:
        copy.wait()
    groups = LANES // n
    per_group = bins // groups
    field = jnp.where(row >= 4, row - 4, 3)
    sums = pair_sums(
        d,
        n,
        bins,
        lambda k: own_side(own[k], norms[k : k + 1, :], row),
        stack,
        weighted,
        offset,
        mask,
    )
    total = jnp.zeros((8, LANES), F32)
    for k in range(bins):
        block = own[k]
        force = contact_force(block, sums[k])
        occupied = jnp.where(lane < counts[k], step_sub, 0.0)
        new_vel = block + occupied * (force - drag_rate * block)
        new_pos = block + occupied * pltpu.roll(new_vel, 4, 0)
        result = jnp.where(row < 3, new_pos, jnp.where(row == 3, block, new_vel))
        moved[k] = result
        load = jnp.where(row == 3, block, block[3:4] * (block + new_vel))
        column = jnp.sum(load, axis=1, keepdims=True)
        base = slot_lane(0, k, n, bins)
        place = (lane == base + per_group * field) & (row >= 3) & (row < 7)
        total = total + jnp.where(place, column, 0.0)
    deposit[...] = jnp.broadcast_to(jnp.sum(total, axis=0, keepdims=True), (8, LANES))


def second_body(
    n, own, before, after, recv, *refs
):
    copies = fetch(refs[0:3], refs[9:12], refs[12])
    pos, vel, stack, weighted, norms, state, counts, offset, mask = refs[3:12]
    bins = own.shape[0]
    d = flat_id()
    row = iota((8, LANES), 0)
    lane = iota((8, LANES), 1)
    seen = recv[0]
    for s in range(1, n):
        seen = seen + recv[s]
    columns = [
        jnp.transpose(jnp.broadcast_to(seen[part : part + 1], (LANES, LANES)))
        for part in range(3)
    ]
    rate = jnp.where(row < 4, step_sub * step_sub, step_sub) * drag_rate

    def push(part, k):
        pair = columns[part][8 * (k // 2) : 8 * (k // 2) + 8]
        other = pltpu.roll(pair, 4, 0)
        here = (row < 4) if k % 2 == 0 else (row >= 4)
        both = jnp.where(here, pair, other)
        return jnp.where((row == 3) | (row == 7), 0.0, both * rate), both

    for k in range(bins):
        load_block(before[k] + push(0, k)[0], row, k, stack, weighted)
        load_block(after[k] + push(2, k)[0], row, 2 * bins + k, stack, weighted)
    for copy in copies:
        copy.wait()
    for k in range(bins):
        block = own[k] + jnp.where(lane < counts[k], push(1, k)[0], 0.0)
        state[k] = block
        norms[k : k + 1, :] = load_block(block, row, bins + k, stack, weighted)
    weighted[3 * bins] = jnp.zeros((16, LANES), BF16)
    sums = pair_sums(
        d,
        n,
        bins,
        lambda k: own_side(state[k], norms[k : k + 1, :], row),
        stack,
        weighted,
        offset,
        mask,
    )
    for k in range(bins):
        block = state[k]
        force = contact_force(block, sums[k])
        occupied = jnp.where(lane < counts[k], step_sub, 0.0)
        fluid_seen = push(1, k)[1]
        new_vel = block + occupied * (force + drag_rate * (fluid_seen - block))
        new_pos = block + occupied * pltpu.roll(new_vel, 4, 0)
        for c in range(3):
            pos[c, k : k + 1, :] = new_pos[c : c + 1]
            vel[c, k : k + 1, :] = new_vel[c + 4 : c + 5]


def side_body(fluid, from_low, from_high, low, high):
    cx, cy = fluid.shape[1:3]
    gx = lax.axis_index("gx")
    has_low = jnp.where(gx > 0, 1.0, 0.0)
    has_high = jnp.where(gx < lax.axis_size("gx") - 1, 1.0, 0.0)
    for j in range(2):
        for c in range(3):
            for i in range(cx + 2):
                at = (j * 3 + c) * (cx + 2) + i
                for out, y in ((low, j), (high, cy - 2 + j)):
                    if i == 0:
                        line = from_low[c, 1, y : y + 1, :] * has_low
                    elif i == cx + 1:
                        line = from_high[c, 0, y : y + 1, :] * has_high
                    else:
                        line = fluid[c, i - 1, y : y + 1, :]
                    out[at : at + 1, :] = line
    used = 6 * (cx + 2)
    if used < low.shape[0]:
        low[used:, :] = jnp.zeros((low.shape[0] - used, LANES), F32)
        high[used:, :] = jnp.zeros((low.shape[0] - used, LANES), F32)


def laplace(at, x):
    centre = at(x)
    tall, wide = centre.shape
    total = at(x + 1) + at(x - 1)
    total = total + pltpu.roll(centre, 1, 0) + pltpu.roll(centre, tall - 1, 0)
    total = total + pltpu.roll(centre, 1, 1) + pltpu.roll(centre, wide - 1, 1)
    return viscosity * (total - 6.0 * centre)


def stencil_body(
    n, fluid, x_low, x_high, y_low, y_high, recv, around, part, faces, rates
):
    cx, cy, cz = fluid.shape[1:]
    gx, gy, gz = (lax.axis_index(a) for a in AXES)
    nx, ny, nz = (lax.axis_size(a) for a in AXES)
    tall, wide = 2 * cy, 2 * cz
    deep = cx + 4

    def exists(dx, dy, dz):
        ok = (gx + dx >= 0) & (gx + dx < nx) & (gy + dy >= 0) & (gy + dy < ny)
        return ok & (gz + dz >= 0) & (gz + dz < nz)

    def chunk(dx, dy, dz):
        source = ((gx + dx) * ny + gy + dy) * nz + gz + dz
        value = recv[jnp.clip(source, 0, n - 1)]
        return jnp.where(exists(dx, dy, dz), value, 0.0)

    def columns(dx, dy):
        above, below = chunk(dx, dy, 1), chunk(dx, dy, -1)
        faces[...] = jnp.zeros((LANES, LANES), F32)
        faces[0:2, :] = above[1:3]
        faces[cz - 2 : cz, :] = below[3:5]
        return jnp.transpose(faces[...])

    own_z = columns(0, 0)
    low_z, high_z = columns(-1, 0), columns(1, 0)
    left_z, right_z = columns(0, -1), columns(0, 1)
    x_on = [jnp.where(exists(-1, 0, 0), 1.0, 0.0), jnp.where(exists(1, 0, 0), 1.0, 0.0)]
    y_on = [jnp.where(exists(0, -1, 0), 1.0, 0.0), jnp.where(exists(0, 1, 0), 1.0, 0.0)]
    row = iota((cy, cz), 0)

    def y_line(ref, j, c, i):
        at = (j * 3 + c) * (cx + 2) + i
        return ref[at : at + 1, :]

    for c in range(3):
        for x in range(-2, cx + 2):
            if x < 0:
                core = x_low[c, x + 2] * x_on[0]
            elif x >= cx:
                core = x_high[c, x - cx] * x_on[1]
            else:
                core = fluid[c, x]
            beyond = jnp.zeros((cy, cz), F32)
            if 0 <= x < cx:
                at = (c * cx + x) * cy
                beyond = own_z[at : at + cy]
            elif x == -1:
                at = (c * cx + cx - 1) * cy
                beyond = low_z[at : at + cy]
            elif x == cx:
                at = c * cx * cy
                beyond = high_z[at : at + cy]
            around[c, x % deep, 0:cy, 0:cz] = core
            around[c, x % deep, 0:cy, cz:wide] = beyond
            side = jnp.zeros((cy, cz), F32)
            side_z = jnp.zeros((cy, cz), F32)
            if -1 <= x <= cx:
                side = jnp.where(row == 0, y_line(y_high, 0, c, x + 1) * y_on[1], side)
                side = jnp.where(row == 1, y_line(y_high, 1, c, x + 1) * y_on[1], side)
                side = jnp.where(row == cy - 2, y_line(y_low, 0, c, x + 1) * y_on[0], side)
                side = jnp.where(row == cy - 1, y_line(y_low, 1, c, x + 1) * y_on[0], side)
            if 0 <= x < cx:
                at = (c * cx + x) * cy
                side_z = jnp.where(row == 0, right_z[at : at + 1], side_z)
                side_z = jnp.where(row == cy - 1, left_z[at + cy - 1 : at + cy], side_z)
            around[c, x % deep, cy:tall, 0:cz] = side
            around[c, x % deep, cy:tall, cz:wide] = side_z

    y_row, z_lane = iota((tall, wide), 0), iota((tall, wide), 1)
    inside = jnp.where(y_row < cy, 1.0, 0.0)
    inside = jnp.where(y_row == cy, y_on[1], jnp.where(y_row == tall - 1, y_on[0], inside))
    deep_on = jnp.where(z_lane < cz, 1.0, 0.0)
    deep_on = jnp.where(z_lane == cz, jnp.where(exists(0, 0, 1), 1.0, 0.0), deep_on)
    deep_on = jnp.where(z_lane == wide - 1, jnp.where(exists(0, 0, -1), 1.0, 0.0), deep_on)
    inside = inside * deep_on
    for c in range(3):
        for x in range(-1, cx + 1):
            rate = laplace(lambda i: around[c, i % deep], x) * inside
            if x < 0:
                rate = rate * x_on[0]
            elif x == cx:
                rate = rate * x_on[1]
            rates[c, x + 1] = rate
        for x in range(cx):
            again = laplace(lambda i: rates[c, i + 1], x)
            total = around[c, x] + rates[c, x + 1] + 0.5 * again
            part[c, x] = total[0:cy, 0:cz]


def deposit_body(n, bins, part, around, ids, recv, out, table, low_table, depth, field):
    cx, cy, cz = part.shape[1:]
    deep = cx + 4
    tall, wide = 2 * cy, 2 * cz
    groups = LANES // n
    per_group = bins // groups
    planes = (cx + 2) * tall

    def packed(ref, which):
        turned = jnp.transpose(
            jnp.concatenate(
                [ref[:, which, :]] + ([jnp.zeros((LANES - n, LANES), F32)] if n < LANES else []), 0
            )
        )
        span = LANES // groups
        total = turned[0:span]
        for g in range(1, groups):
            total = total + pltpu.roll(turned[g * span : (g + 1) * span], g * n, 1)
        return total

    where = packed(ids, 0)
    loads = packed(recv, 3)
    x = where[0:per_group] - (lax.axis_index("gx") * cx - 1).astype(F32)
    y = where[per_group : 2 * per_group] - (lax.axis_index("gy") * cy).astype(F32)
    z = where[2 * per_group : 3 * per_group] - (lax.axis_index("gz") * cz).astype(F32)
    near = (x >= 0) & (x < cx + 2) & (y >= -1) & (y <= cy) & (z >= -1) & (z <= cz)
    y = jnp.where(y < 0, y + tall, y)
    z = jnp.where(z < 0, z + wide, z)
    plane_code = jnp.where(near, x * tall + y, -1.0).astype(jnp.int32)
    depth_code = jnp.where(near, z, -1.0).astype(jnp.int32)
    plane_row = iota((planes, LANES), 0)
    depth_row = iota((wide, LANES), 0)
    for r in range(per_group):
        at = r * LANES
        hit = plane_code[r : r + 1] == plane_row
        for f in range(4):
            load = loads[f * per_group + r : f * per_group + r + 1]
            high, low = pieces_2(load)
            table[f * planes : (f + 1) * planes, at : at + LANES] = jnp.where(
                hit, high, 0.0
            ).astype(BF16)
            low_table[f * planes : (f + 1) * planes, at : at + LANES] = jnp.where(
                hit, low, 0.0
            ).astype(BF16)
        depth[:, at : at + LANES] = jnp.where(
            depth_code[r : r + 1] == depth_row, 1.0, 0.0
        ).astype(BF16)
    spread = nt(table[...], depth[...]) + nt(low_table[...], depth[...])
    factor = coupling * drag_rate * (2.0 - step_sub * drag_rate)
    for c in range(3):
        for i in range(cx + 2):
            moment = spread[c * planes + i * tall : c * planes + (i + 1) * tall]
            mass = spread[3 * planes + i * tall : 3 * planes + (i + 1) * tall]
            field[c, i] = (coupling * drag_rate) * moment - factor * around[
                c, (i - 1) % deep
            ] * mass
        for x in range(cx):
            rate = laplace(lambda i: field[c, i + 1], x)
            total = field[c, x + 1] + 0.5 * rate
            out[c, x] = part[c, x] + total[0:cy, 0:cz]


def ring(n, step):
    return [(i, (i + step) % n) for i in range(n)]


def step(positions, velocities, weights, counts, link_offset, link_mask, bin_box, bin_cell, fluid):
    n = lax.axis_size(AXES)
    nx, ny = lax.axis_size("gx"), lax.axis_size("gy")
    bins = positions.shape[1]
    cx, cy, cz = fluid.shape[1:]
    offset, mask = link_offset.T, link_mask.T
    side_rows = -(-6 * (cx + 2) // 8) * 8

    own, send, face_low, face_high = call(
        functools.partial(prep_body, n),
        [(bins, 8, LANES), (n, 8, LANES), (3, 2, cy, cz), (3, 2, cy, cz)],
        [HBM] * 7,
        [
            pltpu.VMEM(positions.shape, F32),
            pltpu.VMEM(velocities.shape, F32),
            pltpu.VMEM(weights.shape, F32),
            pltpu.VMEM(fluid.shape, F32),
            pltpu.SMEM((bins,), jnp.int32),
            pltpu.SMEM((bins,), jnp.int32),
            pltpu.SMEM((bins,), jnp.int32),
            pltpu.SemaphoreType.DMA((7,)),
        ],
    )(*[
        pltpu.with_memory_space_constraint(value, pltpu.HBM)
        for value in (positions, velocities, weights, fluid, counts, bin_box[:, 0], bin_cell)
    ])
    ids = lax.all_to_all(send, AXES, 0, 0, tiled=True)
    before = lax.ppermute(own, AXES, ring(n, 1))
    after = lax.ppermute(own, AXES, ring(n, -1))
    x_low = lax.ppermute(face_high, "gx", ring(nx, 1))
    x_high = lax.ppermute(face_low, "gx", ring(nx, -1))

    pair_scratch = [
        pltpu.VMEM((3 * bins + 1, 48, LANES), BF16),
        pltpu.VMEM((3 * bins + 1, 16, LANES), BF16),
    ]
    scalars = [
        pltpu.SMEM((bins,), jnp.int32),
        pltpu.SMEM(offset.shape, jnp.int32),
        pltpu.SMEM(mask.shape, jnp.int32),
        pltpu.SemaphoreType.DMA((3,)),
    ]
    moved, deposit = call(
        functools.partial(first_body, n),
        [(bins, 8, LANES), (8, LANES)],
        [VMEM] * 3 + [ANY] * 3,
        pair_scratch + [pltpu.VMEM((bins, LANES), F32)] + scalars,
    )(own, before, after, counts, offset, mask)
    (send,) = call(functools.partial(gather_body, n, bins), [(n, 4, LANES)], [VMEM] * 3)(
        ids, fluid, deposit
    )
    replies = lax.all_to_all(send, AXES, 0, 0, tiled=True)
    before = lax.ppermute(moved, AXES, ring(n, 1))
    after = lax.ppermute(moved, AXES, ring(n, -1))

    side_low, side_high = call(side_body, [(side_rows, LANES)] * 2, [VMEM] * 3)(
        fluid, x_low, x_high
    )
    y_low = lax.ppermute(side_high, "gy", ring(ny, 1))
    y_high = lax.ppermute(side_low, "gy", ring(ny, -1))
    around, part = call(
        functools.partial(stencil_body, n),
        [(3, cx + 4, 2 * cy, 2 * cz), (3, cx, cy, cz)],
        [VMEM] * 6,
        [pltpu.VMEM((LANES, LANES), F32), pltpu.VMEM((3, cx + 2, 2 * cy, 2 * cz), F32)],
    )(fluid, x_low, x_high, y_low, y_high, ids)
    positions_out, velocities_out = call(
        functools.partial(second_body, n),
        [positions.shape, velocities.shape],
        [VMEM] * 4 + [ANY] * 3,
        pair_scratch
        + [pltpu.VMEM((bins, LANES), F32), pltpu.VMEM((bins, 8, LANES), F32)]
        + scalars,
    )(moved, before, after, replies, counts, offset, mask)
    lanes = bins * n
    planes = (cx + 2) * 2 * cy
    (fluid_out,) = call(
        functools.partial(deposit_body, n, bins),
        [fluid.shape],
        [VMEM] * 4,
        [
            pltpu.VMEM((4 * planes, lanes), BF16),
            pltpu.VMEM((4 * planes, lanes), BF16),
            pltpu.VMEM((2 * cz, lanes), BF16),
            pltpu.VMEM((3, cx + 2, 2 * cy, 2 * cz), F32),
        ],
    )(part, around, ids, replies)
    return positions_out, velocities_out, fluid_out


def solution(mesh):
    in_specs = (
        P(None, AXES, None),
        P(None, AXES, None),
        P(AXES, None),
        P(AXES),
        P(AXES, None),
        P(AXES, None),
        P(AXES, None),
        P(AXES),
        P(None, "gx", "gy", "gz"),
    )
    out_specs = (
        P(None, AXES, None),
        P(None, AXES, None),
        P(None, "gx", "gy", "gz"),
    )
    return jax.shard_map(step, mesh=mesh, in_specs=in_specs, out_specs=out_specs, check_vma=False)
```

```python
import functools

import jax
import jax.numpy as jnp
from jax import lax
from jax.experimental import pallas as pl
from jax.experimental.pallas import tpu as pltpu
from jax.sharding import PartitionSpec as P


step_sub = 0.1
stiffness = 0.05
damping = 0.05
drag_rate = 1.0
coupling = 0.004
viscosity = 0.12
log2e = 1.4426950408889634

AXES = ("gx", "gy", "gz")
F32 = jnp.float32
BF16 = jnp.bfloat16
VMEM = pl.BlockSpec(memory_space=pltpu.VMEM)
ANY = pl.BlockSpec(memory_space=pl.ANY)
HBM = pl.BlockSpec(memory_space=pltpu.HBM)
LANES = 128


def iota(shape, dim):
    return lax.broadcasted_iota(jnp.int32, shape, dim)


def nt(a, b, precision=None):
    return lax.dot_general(
        a, b, (((1,), (1,)), ((), ())), preferred_element_type=F32, precision=precision
    )


def tn(a, b):
    return lax.dot_general(a, b, (((0,), (0,)), ((), ())), preferred_element_type=F32)


def nn(a, b):
    return jnp.dot(a, b, preferred_element_type=F32)


def pieces_2(value):
    high = value.astype(BF16).astype(F32)
    return high, value - high


def pieces_3(value):
    high = value.astype(BF16).astype(F32)
    rest = value - high
    middle = rest.astype(BF16).astype(F32)
    return high, middle, rest - middle


def call(body, outs, ins, scratch=(), cost=None):
    return pl.pallas_call(
        body,
        out_shape=[jax.ShapeDtypeStruct(shape, F32) for shape in outs],
        in_specs=ins,
        out_specs=[VMEM] * len(outs),
        scratch_shapes=scratch,
        compiler_params=pltpu.CompilerParams(vmem_limit_bytes=24 * 1024 * 1024),
        cost_estimate=cost,
    )


def slot_lane(field, slot, n, bins):
    groups = LANES // n
    per_group = bins // groups
    return (slot // per_group) * (LANES // groups) + field * per_group + slot % per_group


def fetch(sources, targets, sems):
    copies = [
        pltpu.make_async_copy(source, target, sems.at[i])
        for i, (source, target) in enumerate(zip(sources, targets))
    ]
    for copy in copies:
        copy.start()
    return copies


def exists(dx, dy, dz):
    ok = None
    for axis, step in zip(AXES, (dx, dy, dz)):
        at = lax.axis_index(axis) + step
        here = (at >= 0) & (at < lax.axis_size(axis))
        ok = here if ok is None else ok & here
    return ok


def neighbour_id(dx, dy, dz):
    gx, gy, gz = (lax.axis_index(axis) for axis in AXES)
    return ((gx + dx) * lax.axis_size("gy") + gy + dy) * lax.axis_size("gz") + gz + dz


def prep_body(n, *refs):
    sources, locals_, sems = refs[:7], refs[12:19], refs[19]
    up, down, send, face_low, face_high = refs[7:12]
    copies = fetch(sources, locals_, sems)
    pos, vel, weights, fluid, counts, box, cell = locals_
    for copy in copies:
        copy.wait()
    bins = pos.shape[1]
    cx, cy, cz = fluid.shape[1:]
    lane = iota((8, LANES), 1)
    row = iota((8, LANES), 0)
    for k in range(bins):
        for c in range(3):
            up[k, c : c + 1, :] = pos[c, k : k + 1, :]
            up[k, c + 4 : c + 5, :] = vel[c, k : k + 1, :]
        occupied = iota((1, LANES), 1) < counts[k]
        up[k, 3:4, :] = jnp.where(occupied, weights[k : k + 1, :], 0.0)
        up[k, 7:8, :] = jnp.zeros((1, LANES), F32)
    for k in range(bins):
        down[k] = up[k]
    for out, y in ((down, 0), (up, cy - 2)):
        for c in range(3):
            for x in range(cx):
                at = (c * cx + x) * 2
                out[bins + at // 8, at % 8 : at % 8 + 2, :] = fluid[c, x, y : y + 2, :]
    gy_count = lax.axis_size("gy")
    height = lax.axis_index("gz")
    ids = jnp.zeros((8, LANES), F32)
    for k in range(bins):
        target, inside = box[k], cell[k]
        x = lax.div(target, gy_count) * cx + lax.div(inside, cy * cz)
        y = lax.rem(target, gy_count) * cy + lax.rem(lax.div(inside, cz), cy)
        z = height * cz + lax.rem(inside, cz)
        for field, value in enumerate((x, y, z)):
            ids = jnp.where(lane == slot_lane(field, k, n, bins), value.astype(F32), ids)
    pick = jnp.where(
        ((row == 1) & (lane == 0))
        | ((row == 2) & (lane == 1))
        | ((row == 3) & (lane == cz - 2))
        | ((row == 4) & (lane == cz - 1)),
        1.0,
        0.0,
    )
    flat = fluid[...].reshape(3 * cx * cy, cz)
    flat = jnp.concatenate([flat, jnp.zeros((LANES - 3 * cx * cy, cz), F32)], 0)
    faces = nt(pick, flat, lax.Precision.HIGHEST)
    chunk = jnp.where(row == 0, ids, faces)
    for d in range(n):
        send[d] = chunk
    for dx in (-1, 1):
        for dy in (-1, 1):

            @pl.when(exists(dx, dy, 0))
            def _(dx=dx, dy=dy):
                x, y = (0 if dx < 0 else cx - 1), (0 if dy < 0 else cy - 1)
                value = chunk
                for c in range(3):
                    value = jnp.where(row == 5 + c, fluid[c, x, y : y + 1, :], value)
                send[neighbour_id(dx, dy, 0)] = value

    face_low[...] = fluid[:, 0:2]
    face_high[...] = fluid[:, cx - 2 : cx]


def gather_body(n, bins, recv, fluid, deposit, send):
    cx, cy, cz = fluid.shape[1:]
    per_group = bins // (LANES // n)
    cells = cx * cy
    ids = recv[:, 0, :]
    x = ids - (lax.axis_index("gx") * cx).astype(F32)
    y = pltpu.roll(ids, LANES - per_group, 1) - (lax.axis_index("gy") * cy).astype(F32)
    z = pltpu.roll(ids, LANES - 2 * per_group, 1) - (lax.axis_index("gz") * cz).astype(F32)
    mine = (x >= 0) & (x < cx) & (y >= 0) & (y < cy) & (z >= 0) & (z < cz)
    column_code = jnp.where(mine, x * cy + y, -1.0).astype(jnp.int32)
    depth_code = jnp.where(mine, z, -1.0).astype(jnp.int32)
    flat = fluid[...].reshape(3 * cells, cz)
    high, low = pieces_2(flat)
    table = jnp.concatenate([high, low, jnp.zeros((256 - 6 * cells, cz), F32)], 0).astype(BF16)
    lane_z = iota((n, cz), 1)
    lane_cell = iota((n, 256), 1) % cells
    one_hot = []
    masks = []
    for k in range(bins):
        at = slot_lane(0, k, n, bins)
        one_hot.append(jnp.where(depth_code[:, at : at + 1] == lane_z, 1.0, 0.0))
        masks.append(column_code[:, at : at + 1] == lane_cell)
    picked = nt(jnp.concatenate(one_hot, 0).astype(BF16), table)
    kept = jnp.where(jnp.concatenate(masks, 0), picked, 0.0).astype(BF16)
    rows = iota((256, LANES), 0)
    fold = jnp.where(
        (rows < 6 * cells) & ((rows // cells) % 3 == iota((256, LANES), 1) % 4), 1.0, 0.0
    ).astype(BF16)
    spread = nn(kept, fold)
    slot_of_lane = iota((n, LANES), 1) // 4
    total = jnp.zeros((n, LANES), F32)
    for k in range(bins):
        total = total + jnp.where(slot_of_lane == k, spread[k * n : (k + 1) * n], 0.0)
    send[:, 0, :] = pltpu.roll(total, 1, 0)
    send[:, 1, :] = total
    send[:, 2, :] = pltpu.roll(total, n - 1, 0)
    send[:, 3, :] = jnp.broadcast_to(deposit[0:1], (n, LANES))


def load_block(block, row, index, stack, weighted):
    square = block * block
    norm = (-0.5 * log2e) * (
        square[0:1] + square[1:2] + square[2:3]
    )
    near = jnp.where(
        row < 3, block, jnp.where(row == 3, norm, jnp.where(row == 4, 1.0, 0.0))
    )
    high, middle, low = pieces_3(near)
    stack[index] = jnp.concatenate([high, high, middle, middle, high, low], 0).astype(BF16)
    carried = block[3:4]
    product = jnp.where(row == 3, carried, jnp.where(row == 7, 0.0, block * carried))
    high, low = pieces_2(product)
    weighted[index] = jnp.concatenate([high, low], 0).astype(BF16)
    return norm


def own_side(block, norm, row):
    own = jnp.where(
        row < 3, block * log2e, jnp.where(row == 3, 1.0, jnp.where(row == 4, norm, 0.0))
    )
    high, middle, low = pieces_3(own)
    return jnp.concatenate([high, middle, high, middle, low, high], 0).astype(BF16)


def pair_sums(d, n, bins, own_of, stack, weighted, offset, mask):
    def exponents(k):
        near = [bins + k]
        heavy = [bins + k]
        for q in range(offset.shape[0]):
            shift = offset[q, k]
            near.append(bins + k + shift)
            whole = d * bins + k + shift
            linked = (mask[q, k] != 0) & (whole >= 0) & (whole < n * bins)
            heavy.append(jnp.where(linked, bins + k + shift, 3 * bins))
        others = jnp.concatenate([stack[index] for index in near], 1)
        masses = jnp.concatenate([weighted[index] for index in heavy], 1)
        return tn(own_of(k), others), masses

    sums = []
    following = exponents(0)
    for k in range(bins):
        value, masses = following
        if k + 1 < bins:
            following = exponents(k + 1)
        kernel = jnp.exp2(value)
        high = kernel.astype(BF16)
        low = (kernel - high.astype(F32)).astype(BF16)
        turned = jnp.transpose(nt(high, masses) + nt(low, masses))
        sums.append(turned[0:8] + turned[8:16])
    return sums


def contact_force(block, sums):
    gap = block * sums[3:4] - sums
    return stiffness * pltpu.roll(gap, 4, 0) - damping * gap


def flat_id():
    return (
        lax.axis_index("gx") * lax.axis_size("gy") + lax.axis_index("gy")
    ) * lax.axis_size("gz") + lax.axis_index("gz")


def first_body(
    n, own, before, after, *refs
):
    copies = fetch(refs[0:3], refs[9:12], refs[12])
    moved, moved_down, deposit, stack, weighted, norms, counts, offset, mask = refs[3:12]
    bins = norms.shape[0]
    d = flat_id()
    row = iota((8, LANES), 0)
    lane = iota((8, LANES), 1)
    for k in range(bins, own.shape[0]):
        moved[k] = before[k]
        moved_down[k] = after[k]
    for k in range(bins):
        load_block(before[k], row, k, stack, weighted)
        norms[k : k + 1, :] = load_block(own[k], row, bins + k, stack, weighted)
        load_block(after[k], row, 2 * bins + k, stack, weighted)
    weighted[3 * bins] = jnp.zeros((16, LANES), BF16)
    for copy in copies:
        copy.wait()
    groups = LANES // n
    per_group = bins // groups
    field = jnp.where(row >= 4, row - 4, 3)
    sums = pair_sums(
        d,
        n,
        bins,
        lambda k: own_side(own[k], norms[k : k + 1, :], row),
        stack,
        weighted,
        offset,
        mask,
    )
    total = jnp.zeros((8, LANES), F32)
    for k in range(bins):
        block = own[k]
        force = contact_force(block, sums[k])
        occupied = jnp.where(lane < counts[k], step_sub, 0.0)
        new_vel = block + occupied * (force - drag_rate * block)
        new_pos = block + occupied * pltpu.roll(new_vel, 4, 0)
        result = jnp.where(row < 3, new_pos, jnp.where(row == 3, block, new_vel))
        moved[k] = result
        moved_down[k] = result
        load = jnp.where(row == 3, block, block[3:4] * (block + new_vel))
        column = jnp.sum(load, axis=1, keepdims=True)
        base = slot_lane(0, k, n, bins)
        place = (lane == base + per_group * field) & (row >= 3) & (row < 7)
        total = total + jnp.where(place, column, 0.0)
    deposit[...] = jnp.broadcast_to(jnp.sum(total, axis=0, keepdims=True), (8, LANES))


def second_body(
    n, own, before, after, recv, *refs
):
    copies = fetch(refs[0:3], refs[9:12], refs[12])
    pos, vel, stack, weighted, norms, state, counts, offset, mask = refs[3:12]
    bins = norms.shape[0]
    d = flat_id()
    row = iota((8, LANES), 0)
    lane = iota((8, LANES), 1)
    seen = recv[0]
    for s in range(1, n):
        seen = seen + recv[s]
    columns = [
        jnp.transpose(jnp.broadcast_to(seen[part : part + 1], (LANES, LANES)))
        for part in range(3)
    ]
    rate = jnp.where(row < 4, step_sub * step_sub, step_sub) * drag_rate

    def push(part, k):
        pair = columns[part][8 * (k // 2) : 8 * (k // 2) + 8]
        other = pltpu.roll(pair, 4, 0)
        here = (row < 4) if k % 2 == 0 else (row >= 4)
        both = jnp.where(here, pair, other)
        return jnp.where((row == 3) | (row == 7), 0.0, both * rate), both

    for k in range(bins):
        load_block(before[k] + push(0, k)[0], row, k, stack, weighted)
        load_block(after[k] + push(2, k)[0], row, 2 * bins + k, stack, weighted)
    for copy in copies:
        copy.wait()
    for k in range(bins):
        block = own[k] + jnp.where(lane < counts[k], push(1, k)[0], 0.0)
        state[k] = block
        norms[k : k + 1, :] = load_block(block, row, bins + k, stack, weighted)
    weighted[3 * bins] = jnp.zeros((16, LANES), BF16)
    sums = pair_sums(
        d,
        n,
        bins,
        lambda k: own_side(state[k], norms[k : k + 1, :], row),
        stack,
        weighted,
        offset,
        mask,
    )
    for k in range(bins):
        block = state[k]
        force = contact_force(block, sums[k])
        occupied = jnp.where(lane < counts[k], step_sub, 0.0)
        fluid_seen = push(1, k)[1]
        new_vel = block + occupied * (force + drag_rate * (fluid_seen - block))
        new_pos = block + occupied * pltpu.roll(new_vel, 4, 0)
        for c in range(3):
            pos[c, k : k + 1, :] = new_pos[c : c + 1]
            vel[c, k : k + 1, :] = new_vel[c + 4 : c + 5]


def laplace(at, x):
    centre = at(x)
    tall, wide = centre.shape
    total = at(x + 1) + at(x - 1)
    total = total + pltpu.roll(centre, 1, 0) + pltpu.roll(centre, tall - 1, 0)
    total = total + pltpu.roll(centre, 1, 1) + pltpu.roll(centre, wide - 1, 1)
    return viscosity * (total - 6.0 * centre)


def stencil_body(
    n, base, fluid, x_low, x_high, y_low, y_high, recv, around, part, faces, rates
):
    cx, cy, cz = fluid.shape[1:]
    tall, wide = 2 * cy, 2 * cz
    deep = cx + 4

    def chunk(dx, dy, dz):
        value = recv[jnp.clip(neighbour_id(dx, dy, dz), 0, n - 1)]
        return jnp.where(exists(dx, dy, dz), value, 0.0)

    def columns(dx, dy):
        above, below = chunk(dx, dy, 1), chunk(dx, dy, -1)
        faces[...] = jnp.zeros((LANES, LANES), F32)
        faces[0:2, :] = above[1:3]
        faces[cz - 2 : cz, :] = below[3:5]
        return jnp.transpose(faces[...])

    own_z = columns(0, 0)
    low_z, high_z = columns(-1, 0), columns(1, 0)
    left_z, right_z = columns(0, -1), columns(0, 1)
    x_on = [jnp.where(exists(-1, 0, 0), 1.0, 0.0), jnp.where(exists(1, 0, 0), 1.0, 0.0)]
    y_on = [jnp.where(exists(0, -1, 0), 1.0, 0.0), jnp.where(exists(0, 1, 0), 1.0, 0.0)]
    row = iota((cy, cz), 0)

    corners = {(dx, dy): chunk(dx, dy, 0) for dx in (-1, 1) for dy in (-1, 1)}

    def y_line(ref, j, c, x):
        at = (c * cx + x) * 2 + j
        return ref[base + at // 8, at % 8 : at % 8 + 1, :]

    for c in range(3):
        for x in range(-2, cx + 2):
            if x < 0:
                core = x_low[c, x + 2] * x_on[0]
            elif x >= cx:
                core = x_high[c, x - cx] * x_on[1]
            else:
                core = fluid[c, x]
            beyond = jnp.zeros((cy, cz), F32)
            if 0 <= x < cx:
                at = (c * cx + x) * cy
                beyond = own_z[at : at + cy]
            elif x == -1:
                at = (c * cx + cx - 1) * cy
                beyond = low_z[at : at + cy]
            elif x == cx:
                at = c * cx * cy
                beyond = high_z[at : at + cy]
            around[c, x % deep, 0:cy, 0:cz] = core
            around[c, x % deep, 0:cy, cz:wide] = beyond
            side = jnp.zeros((cy, cz), F32)
            side_z = jnp.zeros((cy, cz), F32)
            if 0 <= x < cx:
                side = jnp.where(row == 0, y_line(y_high, 0, c, x) * y_on[1], side)
                side = jnp.where(row == 1, y_line(y_high, 1, c, x) * y_on[1], side)
                side = jnp.where(row == cy - 2, y_line(y_low, 0, c, x) * y_on[0], side)
                side = jnp.where(row == cy - 1, y_line(y_low, 1, c, x) * y_on[0], side)
            elif x in (-1, cx):
                dx = -1 if x < 0 else 1
                side = jnp.where(row == 0, corners[dx, 1][5 + c : 6 + c], side)
                side = jnp.where(row == cy - 1, corners[dx, -1][5 + c : 6 + c], side)
            if 0 <= x < cx:
                at = (c * cx + x) * cy
                side_z = jnp.where(row == 0, right_z[at : at + 1], side_z)
                side_z = jnp.where(row == cy - 1, left_z[at + cy - 1 : at + cy], side_z)
            around[c, x % deep, cy:tall, 0:cz] = side
            around[c, x % deep, cy:tall, cz:wide] = side_z

    y_row, z_lane = iota((tall, wide), 0), iota((tall, wide), 1)
    inside = jnp.where(y_row < cy, 1.0, 0.0)
    inside = jnp.where(y_row == cy, y_on[1], jnp.where(y_row == tall - 1, y_on[0], inside))
    deep_on = jnp.where(z_lane < cz, 1.0, 0.0)
    deep_on = jnp.where(z_lane == cz, jnp.where(exists(0, 0, 1), 1.0, 0.0), deep_on)
    deep_on = jnp.where(z_lane == wide - 1, jnp.where(exists(0, 0, -1), 1.0, 0.0), deep_on)
    inside = inside * deep_on
    for c in range(3):
        for x in range(-1, cx + 1):
            rate = laplace(lambda i: around[c, i % deep], x) * inside
            if x < 0:
                rate = rate * x_on[0]
            elif x == cx:
                rate = rate * x_on[1]
            rates[c, x + 1] = rate
        for x in range(cx):
            again = laplace(lambda i: rates[c, i + 1], x)
            total = around[c, x] + rates[c, x + 1] + 0.5 * again
            part[c, x] = total[0:cy, 0:cz]


def deposit_body(n, bins, part, around, ids, recv, out, table, low_table, depth, field):
    cx, cy, cz = part.shape[1:]
    deep = cx + 4
    tall, wide = 2 * cy, 2 * cz
    groups = LANES // n
    per_group = bins // groups
    planes = (cx + 2) * tall

    def packed(ref, which):
        turned = jnp.transpose(
            jnp.concatenate(
                [ref[:, which, :]] + ([jnp.zeros((LANES - n, LANES), F32)] if n < LANES else []), 0
            )
        )
        span = LANES // groups
        total = turned[0:span]
        for g in range(1, groups):
            total = total + pltpu.roll(turned[g * span : (g + 1) * span], g * n, 1)
        return total

    where = packed(ids, 0)
    loads = packed(recv, 3)
    x = where[0:per_group] - (lax.axis_index("gx") * cx - 1).astype(F32)
    y = where[per_group : 2 * per_group] - (lax.axis_index("gy") * cy).astype(F32)
    z = where[2 * per_group : 3 * per_group] - (lax.axis_index("gz") * cz).astype(F32)
    near = (x >= 0) & (x < cx + 2) & (y >= -1) & (y <= cy) & (z >= -1) & (z <= cz)
    y = jnp.where(y < 0, y + tall, y)
    z = jnp.where(z < 0, z + wide, z)
    plane_code = jnp.where(near, x * tall + y, -1.0).astype(jnp.int32)
    depth_code = jnp.where(near, z, -1.0).astype(jnp.int32)
    plane_row = iota((planes, LANES), 0)
    depth_row = iota((wide, LANES), 0)
    for r in range(per_group):
        at = r * LANES
        hit = plane_code[r : r + 1] == plane_row
        for f in range(4):
            load = loads[f * per_group + r : f * per_group + r + 1]
            high, low = pieces_2(load)
            table[f * planes : (f + 1) * planes, at : at + LANES] = jnp.where(
                hit, high, 0.0
            ).astype(BF16)
            low_table[f * planes : (f + 1) * planes, at : at + LANES] = jnp.where(
                hit, low, 0.0
            ).astype(BF16)
        depth[:, at : at + LANES] = jnp.where(
            depth_code[r : r + 1] == depth_row, 1.0, 0.0
        ).astype(BF16)
    spread = nt(table[...], depth[...]) + nt(low_table[...], depth[...])
    factor = coupling * drag_rate * (2.0 - step_sub * drag_rate)
    for c in range(3):
        for i in range(cx + 2):
            moment = spread[c * planes + i * tall : c * planes + (i + 1) * tall]
            mass = spread[3 * planes + i * tall : 3 * planes + (i + 1) * tall]
            field[c, i] = (coupling * drag_rate) * moment - factor * around[
                c, (i - 1) % deep
            ] * mass
        for x in range(cx):
            rate = laplace(lambda i: field[c, i + 1], x)
            total = field[c, x + 1] + 0.5 * rate
            out[c, x] = part[c, x] + total[0:cy, 0:cz]


def ring(n, step):
    return [(i, (i + step) % n) for i in range(n)]


def step(positions, velocities, weights, counts, link_offset, link_mask, bin_box, bin_cell, fluid):
    n = lax.axis_size(AXES)
    nx, ny = lax.axis_size("gx"), lax.axis_size("gy")
    bins = positions.shape[1]
    cx, cy, cz = fluid.shape[1:]
    offset, mask = link_offset.T, link_mask.T
    face_blocks = -(-6 * cx // 8)
    relay = lax.axis_size("gz") == 2

    up, down, send, face_low, face_high = call(
        functools.partial(prep_body, n),
        [(bins + face_blocks, 8, LANES)] * 2 + [(n, 8, LANES)] + [(3, 2, cy, cz)] * 2,
        [HBM] * 7,
        [
            pltpu.VMEM(positions.shape, F32),
            pltpu.VMEM(velocities.shape, F32),
            pltpu.VMEM(weights.shape, F32),
            pltpu.VMEM(fluid.shape, F32),
            pltpu.SMEM((bins,), jnp.int32),
            pltpu.SMEM((bins,), jnp.int32),
            pltpu.SMEM((bins,), jnp.int32),
            pltpu.SemaphoreType.DMA((7,)),
        ],
    )(*[
        pltpu.with_memory_space_constraint(value, pltpu.HBM)
        for value in (positions, velocities, weights, fluid, counts, bin_box[:, 0], bin_cell)
    ])
    ids = lax.all_to_all(send, AXES, 0, 0, tiled=True)
    before = lax.ppermute(up, AXES, ring(n, 1))
    after = lax.ppermute(down, AXES, ring(n, -1))
    x_low = lax.ppermute(face_high, "gx", ring(nx, 1))
    x_high = lax.ppermute(face_low, "gx", ring(nx, -1))

    pair_scratch = [
        pltpu.VMEM((3 * bins + 1, 48, LANES), BF16),
        pltpu.VMEM((3 * bins + 1, 16, LANES), BF16),
    ]
    scalars = [
        pltpu.SMEM((bins,), jnp.int32),
        pltpu.SMEM(offset.shape, jnp.int32),
        pltpu.SMEM(mask.shape, jnp.int32),
        pltpu.SemaphoreType.DMA((3,)),
    ]
    moved, moved_down, deposit = call(
        functools.partial(first_body, n),
        [(bins + face_blocks, 8, LANES)] * 2 + [(8, LANES)],
        [VMEM] * 3 + [HBM] * 3,
        pair_scratch + [pltpu.VMEM((bins, LANES), F32)] + scalars,
    )(up, before, after, *[pltpu.with_memory_space_constraint(v, pltpu.HBM) for v in (counts, offset, mask)])
    (send,) = call(functools.partial(gather_body, n, bins), [(n, 4, LANES)], [VMEM] * 3)(
        ids, fluid, deposit
    )
    replies = lax.all_to_all(send, AXES, 0, 0, tiled=True)
    before = lax.ppermute(moved, AXES, ring(n, 1))
    after = lax.ppermute(moved_down, AXES, ring(n, -1))

    y_low, y_high, base = before, after, bins
    if not relay:
        y_low = lax.ppermute(up[bins:], "gy", ring(ny, 1))
        y_high = lax.ppermute(down[bins:], "gy", ring(ny, -1))
        base = 0
    around, part = call(
        functools.partial(stencil_body, n, base),
        [(3, cx + 4, 2 * cy, 2 * cz), (3, cx, cy, cz)],
        [VMEM] * 6,
        [pltpu.VMEM((LANES, LANES), F32), pltpu.VMEM((3, cx + 2, 2 * cy, 2 * cz), F32)],
    )(fluid, x_low, x_high, y_low, y_high, ids)
    positions_out, velocities_out = call(
        functools.partial(second_body, n),
        [positions.shape, velocities.shape],
        [VMEM] * 4 + [HBM] * 3,
        pair_scratch
        + [pltpu.VMEM((bins, LANES), F32), pltpu.VMEM((bins, 8, LANES), F32)]
        + scalars,
    )(moved, before, after, replies, *[pltpu.with_memory_space_constraint(v, pltpu.HBM) for v in (counts, offset, mask)])
    lanes = bins * n
    planes = (cx + 2) * 2 * cy
    (fluid_out,) = call(
        functools.partial(deposit_body, n, bins),
        [fluid.shape],
        [VMEM] * 4,
        [
            pltpu.VMEM((4 * planes, lanes), BF16),
            pltpu.VMEM((4 * planes, lanes), BF16),
            pltpu.VMEM((2 * cz, lanes), BF16),
            pltpu.VMEM((3, cx + 2, 2 * cy, 2 * cz), F32),
        ],
    )(part, around, ids, replies)
    return positions_out, velocities_out, fluid_out


def solution(mesh):
    in_specs = (
        P(None, AXES, None),
        P(None, AXES, None),
        P(AXES, None),
        P(AXES),
        P(AXES, None),
        P(AXES, None),
        P(AXES, None),
        P(AXES),
        P(None, "gx", "gy", "gz"),
    )
    out_specs = (
        P(None, AXES, None),
        P(None, AXES, None),
        P(None, "gx", "gy", "gz"),
    )
    return jax.shard_map(step, mesh=mesh, in_specs=in_specs, out_specs=out_specs, check_vma=False)
```

```python
import functools

import jax
import jax.numpy as jnp
from jax import lax
from jax.experimental import pallas as pl
from jax.experimental.pallas import tpu as pltpu
from jax.sharding import PartitionSpec as P


step_sub = 0.1
stiffness = 0.05
damping = 0.05
drag_rate = 1.0
coupling = 0.004
viscosity = 0.12
log2e = 1.4426950408889634

AXES = ("gx", "gy", "gz")
F32 = jnp.float32
BF16 = jnp.bfloat16
VMEM = pl.BlockSpec(memory_space=pltpu.VMEM)
ANY = pl.BlockSpec(memory_space=pl.ANY)
HBM = pl.BlockSpec(memory_space=pltpu.HBM)
LANES = 128


def iota(shape, dim):
    return lax.broadcasted_iota(jnp.int32, shape, dim)


def nt(a, b, precision=None):
    return lax.dot_general(
        a, b, (((1,), (1,)), ((), ())), preferred_element_type=F32, precision=precision
    )


def tn(a, b):
    return lax.dot_general(a, b, (((0,), (0,)), ((), ())), preferred_element_type=F32)


def nn(a, b):
    return jnp.dot(a, b, preferred_element_type=F32)


def pieces_2(value):
    high = value.astype(BF16).astype(F32)
    return high, value - high


def pieces_3(value):
    high = value.astype(BF16).astype(F32)
    rest = value - high
    middle = rest.astype(BF16).astype(F32)
    return high, middle, rest - middle


def call(body, outs, ins, scratch=(), out_spec=None):
    shapes = [out if isinstance(out[-1], type) else (out, F32) for out in outs]
    return pl.pallas_call(
        body,
        out_shape=[jax.ShapeDtypeStruct(shape, dtype) for shape, dtype in shapes],
        in_specs=ins,
        out_specs=[out_spec or VMEM] * len(outs),
        scratch_shapes=scratch,
        compiler_params=pltpu.CompilerParams(vmem_limit_bytes=24 * 1024 * 1024),
    )


def slot_lane(field, slot, n, bins):
    groups = LANES // n
    per_group = bins // groups
    return (slot // per_group) * (LANES // groups) + field * per_group + slot % per_group


def fetch(sources, targets, sems):
    copies = [
        pltpu.make_async_copy(source, target, sems.at[i])
        for i, (source, target) in enumerate(zip(sources, targets))
    ]
    for copy in copies:
        copy.start()
    return copies


def exists(dx, dy, dz):
    ok = None
    for axis, step in zip(AXES, (dx, dy, dz)):
        at = lax.axis_index(axis) + step
        here = (at >= 0) & (at < lax.axis_size(axis))
        ok = here if ok is None else ok & here
    return ok


def neighbour_id(dx, dy, dz):
    gx, gy, gz = (lax.axis_index(axis) for axis in AXES)
    return ((gx + dx) * lax.axis_size("gy") + gy + dy) * lax.axis_size("gz") + gz + dz


def prep_body(n, *refs):
    sources, locals_, sems = refs[:10], refs[16:26], refs[26]
    up, down, send, face_low, face_high, table = refs[10:16]
    copies = fetch(sources, locals_, sems)
    pos, vel, weights, fluid, counts, box, cell, count_row, offset, mask = locals_
    for copy in copies:
        copy.wait()
    bins = pos.shape[1]
    links = offset.shape[0]
    table[...] = jnp.zeros(table.shape, jnp.int32)
    table[0:1, 0:bins] = count_row[...]
    table[1 : 1 + links, 0:bins] = offset[...]
    table[1 + links : 1 + 2 * links, 0:bins] = mask[...]
    cx, cy, cz = fluid.shape[1:]
    lane = iota((8, LANES), 1)
    row = iota((8, LANES), 0)
    for k in range(bins):
        for c in range(3):
            up[k, c : c + 1, :] = pos[c, k : k + 1, :]
            up[k, c + 4 : c + 5, :] = vel[c, k : k + 1, :]
        occupied = iota((1, LANES), 1) < counts[k]
        up[k, 3:4, :] = jnp.where(occupied, weights[k : k + 1, :], 0.0)
        up[k, 7:8, :] = jnp.zeros((1, LANES), F32)
    for k in range(bins):
        down[k] = up[k]
    for out, y in ((down, 0), (up, cy - 2)):
        for c in range(3):
            for x in range(cx):
                at = (c * cx + x) * 2
                out[bins + at // 8, at % 8 : at % 8 + 2, :] = fluid[c, x, y : y + 2, :]
    gy_count = lax.axis_size("gy")
    height = lax.axis_index("gz")
    ids = jnp.zeros((8, LANES), F32)
    for k in range(bins):
        target, inside = box[k], cell[k]
        x = lax.div(target, gy_count) * cx + lax.div(inside, cy * cz)
        y = lax.rem(target, gy_count) * cy + lax.rem(lax.div(inside, cz), cy)
        z = height * cz + lax.rem(inside, cz)
        for field, value in enumerate((x, y, z)):
            ids = jnp.where(lane == slot_lane(field, k, n, bins), value.astype(F32), ids)
    pick = jnp.where(
        ((row == 1) & (lane == 0))
        | ((row == 2) & (lane == 1))
        | ((row == 3) & (lane == cz - 2))
        | ((row == 4) & (lane == cz - 1)),
        1.0,
        0.0,
    )
    flat = fluid[...].reshape(3 * cx * cy, cz)
    flat = jnp.concatenate([flat, jnp.zeros((LANES - 3 * cx * cy, cz), F32)], 0)
    faces = nt(pick, flat, lax.Precision.HIGHEST)
    chunk = jnp.where(row == 0, ids, faces)
    for d in range(n):
        send[d] = chunk
    for dx in (-1, 1):
        for dy in (-1, 1):

            @pl.when(exists(dx, dy, 0))
            def _(dx=dx, dy=dy):
                x, y = (0 if dx < 0 else cx - 1), (0 if dy < 0 else cy - 1)
                value = chunk
                for c in range(3):
                    value = jnp.where(row == 5 + c, fluid[c, x, y : y + 1, :], value)
                send[neighbour_id(dx, dy, 0)] = value

    face_low[...] = fluid[:, 0:2]
    face_high[...] = fluid[:, cx - 2 : cx]


def gather_body(n, bins, recv, fluid, deposit, send):
    cx, cy, cz = fluid.shape[1:]
    per_group = bins // (LANES // n)
    cells = cx * cy
    ids = recv[:, 0, :]
    x = ids - (lax.axis_index("gx") * cx).astype(F32)
    y = pltpu.roll(ids, LANES - per_group, 1) - (lax.axis_index("gy") * cy).astype(F32)
    z = pltpu.roll(ids, LANES - 2 * per_group, 1) - (lax.axis_index("gz") * cz).astype(F32)
    mine = (x >= 0) & (x < cx) & (y >= 0) & (y < cy) & (z >= 0) & (z < cz)
    column_code = jnp.where(mine, x * cy + y, -1.0).astype(jnp.int32)
    depth_code = jnp.where(mine, z, -1.0).astype(jnp.int32)
    flat = fluid[...].reshape(3 * cells, cz)
    high, low = pieces_2(flat)
    table = jnp.concatenate([high, low, jnp.zeros((256 - 6 * cells, cz), F32)], 0).astype(BF16)
    lane_z = iota((n, cz), 1)
    lane_cell = iota((n, 256), 1) % cells
    one_hot = []
    masks = []
    for k in range(bins):
        at = slot_lane(0, k, n, bins)
        one_hot.append(jnp.where(depth_code[:, at : at + 1] == lane_z, 1.0, 0.0))
        masks.append(column_code[:, at : at + 1] == lane_cell)
    picked = nt(jnp.concatenate(one_hot, 0).astype(BF16), table)
    kept = jnp.where(jnp.concatenate(masks, 0), picked, 0.0).astype(BF16)
    rows = iota((256, LANES), 0)
    fold = jnp.where(
        (rows < 6 * cells) & ((rows // cells) % 3 == iota((256, LANES), 1) % 4), 1.0, 0.0
    ).astype(BF16)
    spread = nn(kept, fold)
    slot_of_lane = iota((n, LANES), 1) // 4
    total = jnp.zeros((n, LANES), F32)
    for k in range(bins):
        total = total + jnp.where(slot_of_lane == k, spread[k * n : (k + 1) * n], 0.0)
    send[:, 0, :] = pltpu.roll(total, 1, 0)
    send[:, 1, :] = total
    send[:, 2, :] = pltpu.roll(total, n - 1, 0)
    send[:, 3, :] = jnp.broadcast_to(deposit[0:1], (n, LANES))


def load_block(block, row, index, stack, weighted):
    square = block * block
    norm = (-0.5 * log2e) * (
        square[0:1] + square[1:2] + square[2:3]
    )
    near = jnp.where(
        row < 3, block, jnp.where(row == 3, norm, jnp.where(row == 4, 1.0, 0.0))
    )
    high, middle, low = pieces_3(near)
    stack[index] = jnp.concatenate([high, high, middle, middle, high, low], 0).astype(BF16)
    carried = block[3:4]
    product = jnp.where(row == 3, carried, jnp.where(row == 7, 0.0, block * carried))
    high, low = pieces_2(product)
    weighted[index] = jnp.concatenate([high, low], 0).astype(BF16)
    return norm


def own_side(block, norm, row):
    own = jnp.where(
        row < 3, block * log2e, jnp.where(row == 3, 1.0, jnp.where(row == 4, norm, 0.0))
    )
    high, middle, low = pieces_3(own)
    return jnp.concatenate([high, middle, high, middle, low, high], 0).astype(BF16)


def pair_sums(d, n, bins, links, own_of, stack, weighted, highs, lows, table):
    for k in range(bins):
        near = [bins + k] + [bins + k + table[1 + q, k] for q in range(links)]
        others = jnp.concatenate([stack[index] for index in near], 1)
        kernel = jnp.exp2(tn(own_of(k), others))
        high = kernel.astype(BF16)
        highs[k] = high
        lows[k] = (kernel - high.astype(F32)).astype(BF16)
    sums = []
    for k in range(bins):
        heavy = [bins + k]
        for q in range(links):
            shift = table[1 + q, k]
            whole = d * bins + k + shift
            linked = (table[1 + links + q, k] != 0) & (whole >= 0) & (whole < n * bins)
            heavy.append(jnp.where(linked, bins + k + shift, 3 * bins))
        masses = jnp.concatenate([weighted[index] for index in heavy], 1)
        turned = jnp.transpose(nt(highs[k], masses) + nt(lows[k], masses))
        sums.append(turned[0:8] + turned[8:16])
    return sums


def contact_force(block, sums):
    gap = block * sums[3:4] - sums
    return stiffness * pltpu.roll(gap, 4, 0) - damping * gap


def flat_id():
    return (
        lax.axis_index("gx") * lax.axis_size("gy") + lax.axis_index("gy")
    ) * lax.axis_size("gz") + lax.axis_index("gz")


def first_body(
    n, links, own, before, after, *refs
):
    copies = fetch(refs[0:1], refs[9:10], refs[10])
    moved, moved_down, deposit, stack, weighted, highs, lows, norms, table = refs[1:10]
    bins = norms.shape[0]
    d = flat_id()
    row = iota((8, LANES), 0)
    lane = iota((8, LANES), 1)
    for k in range(bins, own.shape[0]):
        moved[k] = before[k]
        moved_down[k] = after[k]
    for k in range(bins):
        load_block(before[k], row, k, stack, weighted)
        norms[k : k + 1, :] = load_block(own[k], row, bins + k, stack, weighted)
        load_block(after[k], row, 2 * bins + k, stack, weighted)
    weighted[3 * bins] = jnp.zeros((16, LANES), BF16)
    for copy in copies:
        copy.wait()
    groups = LANES // n
    per_group = bins // groups
    field = jnp.where(row >= 4, row - 4, 3)
    sums = pair_sums(
        d,
        n,
        bins,
        links,
        lambda k: own_side(own[k], norms[k : k + 1, :], row),
        stack,
        weighted,
        highs,
        lows,
        table,
    )
    total = jnp.zeros((8, LANES), F32)
    for k in range(bins):
        block = own[k]
        force = contact_force(block, sums[k])
        occupied = jnp.where(lane < table[0, k], step_sub, 0.0)
        new_vel = block + occupied * (force - drag_rate * block)
        new_pos = block + occupied * pltpu.roll(new_vel, 4, 0)
        result = jnp.where(row < 3, new_pos, jnp.where(row == 3, block, new_vel))
        moved[k] = result
        moved_down[k] = result
        load = jnp.where(row == 3, block, block[3:4] * (block + new_vel))
        column = jnp.sum(load, axis=1, keepdims=True)
        base = slot_lane(0, k, n, bins)
        place = (lane == base + per_group * field) & (row >= 3) & (row < 7)
        total = total + jnp.where(place, column, 0.0)
    deposit[...] = jnp.broadcast_to(jnp.sum(total, axis=0, keepdims=True), (8, LANES))


def final_body(n, links, own, before, after, recv, scalars, part, around, planes, depth, *refs):
    outs, refs = refs[0:3], refs[3:]
    stack, weighted, highs, lows, norms, state, table, pos, vel, fluid = refs[0:10]
    copies = fetch([scalars], [table], refs[10])
    deposit(n, norms.shape[0], part, around, planes, depth, recv, fluid, *refs[12:15])
    written = fetch([fluid], outs[2:3], refs[11].at[2:3])
    bins = norms.shape[0]
    d = flat_id()
    row = iota((8, LANES), 0)
    lane = iota((8, LANES), 1)
    seen = recv[0]
    for s in range(1, n):
        seen = seen + recv[s]
    columns = [
        jnp.transpose(jnp.broadcast_to(seen[part : part + 1], (LANES, LANES)))
        for part in range(3)
    ]
    rate = jnp.where(row < 4, step_sub * step_sub, step_sub) * drag_rate

    def push(part, k):
        pair = columns[part][8 * (k // 2) : 8 * (k // 2) + 8]
        other = pltpu.roll(pair, 4, 0)
        here = (row < 4) if k % 2 == 0 else (row >= 4)
        both = jnp.where(here, pair, other)
        return jnp.where((row == 3) | (row == 7), 0.0, both * rate), both

    for k in range(bins):
        load_block(before[k] + push(0, k)[0], row, k, stack, weighted)
        load_block(after[k] + push(2, k)[0], row, 2 * bins + k, stack, weighted)
    for copy in copies:
        copy.wait()
    for k in range(bins):
        block = own[k] + jnp.where(lane < table[0, k], push(1, k)[0], 0.0)
        state[k] = block
        norms[k : k + 1, :] = load_block(block, row, bins + k, stack, weighted)
    weighted[3 * bins] = jnp.zeros((16, LANES), BF16)
    sums = pair_sums(
        d,
        n,
        bins,
        links,
        lambda k: own_side(state[k], norms[k : k + 1, :], row),
        stack,
        weighted,
        highs,
        lows,
        table,
    )
    for k in range(bins):
        block = state[k]
        force = contact_force(block, sums[k])
        occupied = jnp.where(lane < table[0, k], step_sub, 0.0)
        fluid_seen = push(1, k)[1]
        new_vel = block + occupied * (force + drag_rate * (fluid_seen - block))
        new_pos = block + occupied * pltpu.roll(new_vel, 4, 0)
        for c in range(3):
            pos[c, k : k + 1, :] = new_pos[c : c + 1]
            vel[c, k : k + 1, :] = new_vel[c + 4 : c + 5]
    written += fetch([pos, vel], outs[0:2], refs[11])
    for copy in written:
        copy.wait()


def laplace(at, x):
    centre = at(x)
    tall, wide = centre.shape
    total = at(x + 1) + at(x - 1)
    total = total + pltpu.roll(centre, 1, 0) + pltpu.roll(centre, tall - 1, 0)
    total = total + pltpu.roll(centre, 1, 1) + pltpu.roll(centre, wide - 1, 1)
    return viscosity * (total - 6.0 * centre)


def stencil_body(
    n, bins, base, fluid, x_low, x_high, y_low, y_high, recv, around, part, planes, depth, faces, rates
):
    cx, cy, cz = fluid.shape[1:]
    tall, wide = 2 * cy, 2 * cz
    deep = cx + 4

    def chunk(dx, dy, dz):
        value = recv[jnp.clip(neighbour_id(dx, dy, dz), 0, n - 1)]
        return jnp.where(exists(dx, dy, dz), value, 0.0)

    def columns(dx, dy):
        above, below = chunk(dx, dy, 1), chunk(dx, dy, -1)
        faces[...] = jnp.zeros((LANES, LANES), F32)
        faces[0:2, :] = above[1:3]
        faces[cz - 2 : cz, :] = below[3:5]
        return jnp.transpose(faces[...])

    own_z = columns(0, 0)
    low_z, high_z = columns(-1, 0), columns(1, 0)
    left_z, right_z = columns(0, -1), columns(0, 1)
    x_on = [jnp.where(exists(-1, 0, 0), 1.0, 0.0), jnp.where(exists(1, 0, 0), 1.0, 0.0)]
    y_on = [jnp.where(exists(0, -1, 0), 1.0, 0.0), jnp.where(exists(0, 1, 0), 1.0, 0.0)]
    row = iota((cy, cz), 0)

    corners = {(dx, dy): chunk(dx, dy, 0) for dx in (-1, 1) for dy in (-1, 1)}

    def y_line(ref, j, c, x):
        at = (c * cx + x) * 2 + j
        return ref[base + at // 8, at % 8 : at % 8 + 1, :]

    for c in range(3):
        for x in range(-2, cx + 2):
            if x < 0:
                core = x_low[c, x + 2] * x_on[0]
            elif x >= cx:
                core = x_high[c, x - cx] * x_on[1]
            else:
                core = fluid[c, x]
            beyond = jnp.zeros((cy, cz), F32)
            if 0 <= x < cx:
                at = (c * cx + x) * cy
                beyond = own_z[at : at + cy]
            elif x == -1:
                at = (c * cx + cx - 1) * cy
                beyond = low_z[at : at + cy]
            elif x == cx:
                at = c * cx * cy
                beyond = high_z[at : at + cy]
            around[c, x % deep, 0:cy, 0:cz] = core
            around[c, x % deep, 0:cy, cz:wide] = beyond
            side = jnp.zeros((cy, cz), F32)
            side_z = jnp.zeros((cy, cz), F32)
            if 0 <= x < cx:
                side = jnp.where(row == 0, y_line(y_high, 0, c, x) * y_on[1], side)
                side = jnp.where(row == 1, y_line(y_high, 1, c, x) * y_on[1], side)
                side = jnp.where(row == cy - 2, y_line(y_low, 0, c, x) * y_on[0], side)
                side = jnp.where(row == cy - 1, y_line(y_low, 1, c, x) * y_on[0], side)
            elif x in (-1, cx):
                dx = -1 if x < 0 else 1
                side = jnp.where(row == 0, corners[dx, 1][5 + c : 6 + c], side)
                side = jnp.where(row == cy - 1, corners[dx, -1][5 + c : 6 + c], side)
            if 0 <= x < cx:
                at = (c * cx + x) * cy
                side_z = jnp.where(row == 0, right_z[at : at + 1], side_z)
                side_z = jnp.where(row == cy - 1, left_z[at + cy - 1 : at + cy], side_z)
            around[c, x % deep, cy:tall, 0:cz] = side
            around[c, x % deep, cy:tall, cz:wide] = side_z

    y_row, z_lane = iota((tall, wide), 0), iota((tall, wide), 1)
    inside = jnp.where(y_row < cy, 1.0, 0.0)
    inside = jnp.where(y_row == cy, y_on[1], jnp.where(y_row == tall - 1, y_on[0], inside))
    deep_on = jnp.where(z_lane < cz, 1.0, 0.0)
    deep_on = jnp.where(z_lane == cz, jnp.where(exists(0, 0, 1), 1.0, 0.0), deep_on)
    deep_on = jnp.where(z_lane == wide - 1, jnp.where(exists(0, 0, -1), 1.0, 0.0), deep_on)
    inside = inside * deep_on
    for c in range(3):
        for x in range(-1, cx + 1):
            rate = laplace(lambda i: around[c, i % deep], x) * inside
            if x < 0:
                rate = rate * x_on[0]
            elif x == cx:
                rate = rate * x_on[1]
            rates[c, x + 1] = rate
        for x in range(cx):
            again = laplace(lambda i: rates[c, i + 1], x)
            total = around[c, x] + rates[c, x + 1] + 0.5 * again
            part[c, x] = total[0:cy, 0:cz]
    locate(n, bins, (cx, cy, cz), recv, planes, depth)


def packed(n, ref, which):
    groups = LANES // n
    rows = [ref[:, which, :]]
    if n < LANES:
        rows.append(jnp.zeros((LANES - n, LANES), F32))
    turned = jnp.transpose(jnp.concatenate(rows, 0))
    span = LANES // groups
    total = turned[0:span]
    for g in range(1, groups):
        total = total + pltpu.roll(turned[g * span : (g + 1) * span], g * n, 1)
    return total


def locate(n, bins, sizes, ids, planes, depth):
    cx, cy, cz = sizes
    tall, wide = 2 * cy, 2 * cz
    per_group = bins // (LANES // n)
    where = packed(n, ids, 0)
    x = where[0:per_group] - (lax.axis_index("gx") * cx - 1).astype(F32)
    y = where[per_group : 2 * per_group] - (lax.axis_index("gy") * cy).astype(F32)
    z = where[2 * per_group : 3 * per_group] - (lax.axis_index("gz") * cz).astype(F32)
    near = (x >= 0) & (x < cx + 2) & (y >= -1) & (y <= cy) & (z >= -1) & (z <= cz)
    y = jnp.where(y < 0, y + tall, y)
    z = jnp.where(z < 0, z + wide, z)
    planes[...] = jnp.where(near, x * tall + y, -1.0)
    depth_code = jnp.where(near, z, -1.0).astype(jnp.int32)
    depth_row = iota((wide, LANES), 0)
    for r in range(per_group):
        depth[:, r * LANES : (r + 1) * LANES] = jnp.where(
            depth_code[r : r + 1] == depth_row, 1.0, 0.0
        ).astype(BF16)


def deposit(n, bins, part, around, planes, depth, recv, out, table, low_table, field):
    cx, cy, cz = part.shape[1:]
    deep = cx + 4
    tall = 2 * cy
    per_group = bins // (LANES // n)
    count = (cx + 2) * tall
    loads = packed(n, recv, 3)
    plane_code = planes[...].astype(jnp.int32)
    plane_row = iota((count, LANES), 0)
    for r in range(per_group):
        at = r * LANES
        hit = plane_code[r : r + 1] == plane_row
        for f in range(4):
            load = loads[f * per_group + r : f * per_group + r + 1]
            high, low = pieces_2(load)
            table[f * count : (f + 1) * count, at : at + LANES] = jnp.where(
                hit, high, 0.0
            ).astype(BF16)
            low_table[f * count : (f + 1) * count, at : at + LANES] = jnp.where(
                hit, low, 0.0
            ).astype(BF16)
    spread = nt(table[...], depth[...]) + nt(low_table[...], depth[...])
    factor = coupling * drag_rate * (2.0 - step_sub * drag_rate)
    for c in range(3):
        for i in range(cx + 2):
            moment = spread[c * count + i * tall : c * count + (i + 1) * tall]
            mass = spread[3 * count + i * tall : 3 * count + (i + 1) * tall]
            field[c, i] = (coupling * drag_rate) * moment - factor * around[
                c, (i - 1) % deep
            ] * mass
        for x in range(cx):
            rate = laplace(lambda i: field[c, i + 1], x)
            total = field[c, x + 1] + 0.5 * rate
            out[c, x] = part[c, x] + total[0:cy, 0:cz]


def ring(n, step):
    return [(i, (i + step) % n) for i in range(n)]


def step(positions, velocities, weights, counts, link_offset, link_mask, bin_box, bin_cell, fluid):
    n = lax.axis_size(AXES)
    nx, ny = lax.axis_size("gx"), lax.axis_size("gy")
    bins = positions.shape[1]
    cx, cy, cz = fluid.shape[1:]
    offset, mask = link_offset.T, link_mask.T
    face_blocks = -(-6 * cx // 8)
    relay = lax.axis_size("gz") == 2

    links = offset.shape[0]
    up, down, send, face_low, face_high, table = call(
        functools.partial(prep_body, n),
        [(bins + face_blocks, 8, LANES)] * 2
        + [(n, 8, LANES)]
        + [(3, 2, cy, cz)] * 2
        + [((8, LANES), jnp.int32)],
        [HBM] * 10,
        [
            pltpu.VMEM(positions.shape, F32),
            pltpu.VMEM(velocities.shape, F32),
            pltpu.VMEM(weights.shape, F32),
            pltpu.VMEM(fluid.shape, F32),
            pltpu.SMEM((bins,), jnp.int32),
            pltpu.SMEM((bins,), jnp.int32),
            pltpu.SMEM((bins,), jnp.int32),
            pltpu.VMEM((1, bins), jnp.int32),
            pltpu.VMEM(offset.shape, jnp.int32),
            pltpu.VMEM(mask.shape, jnp.int32),
            pltpu.SemaphoreType.DMA((10,)),
        ],
    )(
        *[
            pltpu.with_memory_space_constraint(value, pltpu.HBM)
            for value in (
                positions,
                velocities,
                weights,
                fluid,
                counts,
                bin_box[:, 0],
                bin_cell,
                counts[None],
                offset,
                mask,
            )
        ]
    )
    ids = lax.all_to_all(send, AXES, 0, 0, tiled=True)
    before = lax.ppermute(up, AXES, ring(n, 1))
    after = lax.ppermute(down, AXES, ring(n, -1))
    x_low = lax.ppermute(face_high, "gx", ring(nx, 1))
    x_high = lax.ppermute(face_low, "gx", ring(nx, -1))

    pair_scratch = [
        pltpu.VMEM((3 * bins + 1, 48, LANES), BF16),
        pltpu.VMEM((3 * bins + 1, 16, LANES), BF16),
        pltpu.VMEM((bins, LANES, (offset.shape[0] + 1) * LANES), BF16),
        pltpu.VMEM((bins, LANES, (offset.shape[0] + 1) * LANES), BF16),
    ]
    held = [pltpu.SMEM((8, LANES), jnp.int32)]
    moved, moved_down, deposits = call(
        functools.partial(first_body, n, links),
        [(bins + face_blocks, 8, LANES)] * 2 + [(8, LANES)],
        [VMEM] * 4,
        pair_scratch
        + [pltpu.VMEM((bins, LANES), F32)]
        + held
        + [pltpu.SemaphoreType.DMA((1,))],
    )(up, before, after, table)
    (send,) = call(functools.partial(gather_body, n, bins), [(n, 4, LANES)], [VMEM] * 3)(
        ids, fluid, deposits
    )
    replies = lax.all_to_all(send, AXES, 0, 0, tiled=True)
    before = lax.ppermute(moved, AXES, ring(n, 1))
    after = lax.ppermute(moved_down, AXES, ring(n, -1))

    y_low, y_high, base = before, after, bins
    if not relay:
        y_low = lax.ppermute(up[bins:], "gy", ring(ny, 1))
        y_high = lax.ppermute(down[bins:], "gy", ring(ny, -1))
        base = 0
    lanes = bins * n
    per_group = bins // (LANES // n)
    around, part, planes, depth = call(
        functools.partial(stencil_body, n, bins, base),
        [(3, cx + 4, 2 * cy, 2 * cz), (3, cx, cy, cz), (per_group, LANES), ((2 * cz, lanes), BF16)],
        [VMEM] * 6,
        [pltpu.VMEM((LANES, LANES), F32), pltpu.VMEM((3, cx + 2, 2 * cy, 2 * cz), F32)],
    )(fluid, x_low, x_high, y_low, y_high, ids)
    count = (cx + 2) * 2 * cy
    positions_out, velocities_out, fluid_out = call(
        functools.partial(final_body, n, links),
        [positions.shape, velocities.shape, fluid.shape],
        [VMEM] * 9,
        pair_scratch
        + [pltpu.VMEM((bins, LANES), F32), pltpu.VMEM((bins, 8, LANES), F32)]
        + held
        + [
            pltpu.VMEM(positions.shape, F32),
            pltpu.VMEM(velocities.shape, F32),
            pltpu.VMEM(fluid.shape, F32),
            pltpu.SemaphoreType.DMA((1,)),
            pltpu.SemaphoreType.DMA((3,)),
            pltpu.VMEM((4 * count, lanes), BF16),
            pltpu.VMEM((4 * count, lanes), BF16),
            pltpu.VMEM((3, cx + 2, 2 * cy, 2 * cz), F32),
        ],
        HBM,
    )(moved, before, after, replies, table, part, around, planes, depth)
    return positions_out, velocities_out, fluid_out


def solution(mesh):
    in_specs = (
        P(None, AXES, None),
        P(None, AXES, None),
        P(AXES, None),
        P(AXES),
        P(AXES, None),
        P(AXES, None),
        P(AXES, None),
        P(AXES),
        P(None, "gx", "gy", "gz"),
    )
    out_specs = (
        P(None, AXES, None),
        P(None, AXES, None),
        P(None, "gx", "gy", "gz"),
    )
    return jax.shard_map(step, mesh=mesh, in_specs=in_specs, out_specs=out_specs, check_vma=False)
```

```python
import functools

import jax
import jax.numpy as jnp
from jax import lax
from jax.experimental import pallas as pl
from jax.experimental.pallas import tpu as pltpu
from jax.sharding import PartitionSpec as P


step_sub = 0.1
stiffness = 0.05
damping = 0.05
drag_rate = 1.0
coupling = 0.004
viscosity = 0.12
log2e = 1.4426950408889634

AXES = ("gx", "gy", "gz")
F32 = jnp.float32
BF16 = jnp.bfloat16
VMEM = pl.BlockSpec(memory_space=pltpu.VMEM)
ANY = pl.BlockSpec(memory_space=pl.ANY)
HBM = pl.BlockSpec(memory_space=pltpu.HBM)
LANES = 128


def iota(shape, dim):
    return lax.broadcasted_iota(jnp.int32, shape, dim)


def nt(a, b, precision=None):
    return lax.dot_general(
        a, b, (((1,), (1,)), ((), ())), preferred_element_type=F32, precision=precision
    )


def tn(a, b):
    return lax.dot_general(a, b, (((0,), (0,)), ((), ())), preferred_element_type=F32)


def nn(a, b):
    return jnp.dot(a, b, preferred_element_type=F32)


def pieces_2(value):
    high = value.astype(BF16).astype(F32)
    return high, value - high


def pieces_3(value):
    high = value.astype(BF16).astype(F32)
    rest = value - high
    middle = rest.astype(BF16).astype(F32)
    return high, middle, rest - middle


def call(body, outs, ins, scratch=(), out_spec=None):
    shapes = [out if isinstance(out[-1], type) else (out, F32) for out in outs]
    return pl.pallas_call(
        body,
        out_shape=[jax.ShapeDtypeStruct(shape, dtype) for shape, dtype in shapes],
        in_specs=ins,
        out_specs=out_spec or [VMEM] * len(outs),
        scratch_shapes=scratch,
        compiler_params=pltpu.CompilerParams(vmem_limit_bytes=24 * 1024 * 1024),
    )


def slot_lane(field, slot, n, bins):
    groups = LANES // n
    per_group = bins // groups
    return (slot // per_group) * (LANES // groups) + field * per_group + slot % per_group


def fetch(sources, targets, sems):
    copies = [
        pltpu.make_async_copy(source, target, sems.at[i])
        for i, (source, target) in enumerate(zip(sources, targets))
    ]
    for copy in copies:
        copy.start()
    return copies


def exists(dx, dy, dz):
    ok = None
    for axis, step in zip(AXES, (dx, dy, dz)):
        at = lax.axis_index(axis) + step
        here = (at >= 0) & (at < lax.axis_size(axis))
        ok = here if ok is None else ok & here
    return ok


def neighbour_id(dx, dy, dz):
    gx, gy, gz = (lax.axis_index(axis) for axis in AXES)
    return ((gx + dx) * lax.axis_size("gy") + gy + dy) * lax.axis_size("gz") + gz + dz


def prep_body(n, *refs):
    sources, locals_, sems = refs[:10], refs[16:26], refs[26]
    up, down, sent, face_low, face_high, table = refs[10:16]
    send, sent_sem = refs[27:29]
    copies = fetch(sources, locals_, sems)
    pos, vel, weights, fluid, counts, box, cell, count_row, offset, mask = locals_
    for copy in copies:
        copy.wait()
    bins = pos.shape[1]
    links = offset.shape[0]
    cx, cy, cz = fluid.shape[1:]
    lane = iota((8, LANES), 1)
    row = iota((8, LANES), 0)
    gy_count = lax.axis_size("gy")
    height = lax.axis_index("gz")
    ids = jnp.zeros((8, LANES), F32)
    for k in range(bins):
        target, inside = box[k], cell[k]
        x = lax.div(target, gy_count) * cx + lax.div(inside, cy * cz)
        y = lax.rem(target, gy_count) * cy + lax.rem(lax.div(inside, cz), cy)
        z = height * cz + lax.rem(inside, cz)
        for field, value in enumerate((x, y, z)):
            ids = jnp.where(lane == slot_lane(field, k, n, bins), value.astype(F32), ids)
    flat = fluid[...].reshape(3 * cx * cy, cz)
    flat = jnp.concatenate([flat, jnp.zeros((LANES - 3 * cx * cy, cz), F32)], 0)
    pick = jnp.where(
        ((row == 1) & (lane == 0))
        | ((row == 2) & (lane == 1))
        | ((row == 3) & (lane == cz - 2))
        | ((row == 4) & (lane == cz - 1)),
        1.0,
        0.0,
    )
    pick = jnp.concatenate([pick, jnp.zeros((8, LANES), F32)], 0).astype(BF16)
    faces = nt(pick, jnp.concatenate(pieces_3(flat), 0).astype(BF16))[0:8]
    faces = faces[:, 0:LANES] + faces[:, LANES : 2 * LANES] + faces[:, 2 * LANES :]
    chunk = jnp.where(row == 0, ids, faces)
    for d in range(n):
        send[d] = chunk
    for dx in (-1, 1):
        for dy in (-1, 1):

            @pl.when(exists(dx, dy, 0))
            def _(dx=dx, dy=dy):
                x, y = (0 if dx < 0 else cx - 1), (0 if dy < 0 else cy - 1)
                value = chunk
                for c in range(3):
                    value = jnp.where(row == 5 + c, fluid[c, x, y : y + 1, :], value)
                send[neighbour_id(dx, dy, 0)] = value

    written = fetch([send], [sent], sent_sem)
    for k in range(bins):
        for c in range(3):
            up[k, c : c + 1, :] = pos[c, k : k + 1, :]
            up[k, c + 4 : c + 5, :] = vel[c, k : k + 1, :]
        occupied = iota((1, LANES), 1) < counts[k]
        up[k, 3:4, :] = jnp.where(occupied, weights[k : k + 1, :], 0.0)
        up[k, 7:8, :] = jnp.zeros((1, LANES), F32)
    for k in range(bins):
        down[k] = up[k]
    for out, y in ((down, 0), (up, cy - 2)):
        for c in range(3):
            for x in range(cx):
                at = (c * cx + x) * 2
                out[bins + at // 8, at % 8 : at % 8 + 2, :] = fluid[c, x, y : y + 2, :]
    table[...] = jnp.zeros(table.shape, jnp.int32)
    table[0:1, 0:bins] = count_row[...]
    table[1 : 1 + links, 0:bins] = offset[...]
    table[1 + links : 1 + 2 * links, 0:bins] = mask[...]
    face_low[...] = fluid[:, 0:2]
    face_high[...] = fluid[:, cx - 2 : cx]
    for copy in written:
        copy.wait()


def gather_body(n, bins, recv, fluid, deposit, send):
    cx, cy, cz = fluid.shape[1:]
    per_group = bins // (LANES // n)
    cells = cx * cy
    ids = recv[:, 0, :]
    x = ids - (lax.axis_index("gx") * cx).astype(F32)
    y = pltpu.roll(ids, LANES - per_group, 1) - (lax.axis_index("gy") * cy).astype(F32)
    z = pltpu.roll(ids, LANES - 2 * per_group, 1) - (lax.axis_index("gz") * cz).astype(F32)
    mine = (x >= 0) & (x < cx) & (y >= 0) & (y < cy) & (z >= 0) & (z < cz)
    column_code = jnp.where(mine, x * cy + y, -1.0).astype(jnp.int32)
    depth_code = jnp.where(mine, z, -1.0).astype(jnp.int32)
    flat = fluid[...].reshape(3 * cells, cz)
    high, low = pieces_2(flat)
    table = jnp.concatenate([high, low, jnp.zeros((256 - 6 * cells, cz), F32)], 0).astype(BF16)
    lane_z = iota((n, cz), 1)
    lane_cell = iota((n, 256), 1) % cells
    one_hot = []
    masks = []
    for k in range(bins):
        at = slot_lane(0, k, n, bins)
        one_hot.append(jnp.where(depth_code[:, at : at + 1] == lane_z, 1.0, 0.0))
        masks.append(column_code[:, at : at + 1] == lane_cell)
    picked = nt(jnp.concatenate(one_hot, 0).astype(BF16), table)
    kept = jnp.where(jnp.concatenate(masks, 0), picked, 0.0).astype(BF16)
    rows = iota((256, LANES), 0)
    fold = jnp.where(
        (rows < 6 * cells) & ((rows // cells) % 3 == iota((256, LANES), 1) % 4), 1.0, 0.0
    ).astype(BF16)
    spread = nn(kept, fold)
    span = 8 * per_group
    lane = iota((n, LANES), 1)
    plain_slot = jnp.where(lane < 4 * bins, lane // 4, -1)
    within = lane % span - 4 * per_group
    mixed_slot = jnp.where(within >= 0, lane // span * per_group + within // 4, -1)
    plain = jnp.zeros((n, LANES), F32)
    mixed = jnp.zeros((n, LANES), F32)
    for k in range(bins):
        value = spread[k * n : (k + 1) * n]
        plain = plain + jnp.where(plain_slot == k, value, 0.0)
        mixed = mixed + jnp.where(mixed_slot == k, value, 0.0)
    send[:, 0, :] = pltpu.roll(plain, 1, 0) + pltpu.roll(plain, 4 * bins, 1)
    send[:, 1, :] = pltpu.roll(mixed, n - 1, 0) + deposit[0:1]


def load_block(block, row, index, stack, weighted):
    square = block * block
    norm = (-0.5 * log2e) * (
        square[0:1] + square[1:2] + square[2:3]
    )
    near = jnp.where(
        row < 3, block, jnp.where(row == 3, norm, jnp.where(row == 4, 1.0, 0.0))
    )
    high, middle, low = pieces_3(near)
    stack[index] = jnp.concatenate([high, high, middle, middle, high, low], 0).astype(BF16)
    carried = block[3:4]
    product = jnp.where(row == 3, carried, jnp.where(row == 7, 0.0, block * carried))
    high, low = pieces_2(product)
    weighted[index] = jnp.concatenate([high, low], 0).astype(BF16)
    return norm


def own_side(block, norm, row):
    own = jnp.where(
        row < 3, block * log2e, jnp.where(row == 3, 1.0, jnp.where(row == 4, norm, 0.0))
    )
    high, middle, low = pieces_3(own)
    return jnp.concatenate([high, middle, high, middle, low, high], 0).astype(BF16)


def pair_sums(d, n, bins, links, own_of, stack, weighted, highs, lows, table):
    for k in range(bins):
        near = [bins + k] + [bins + k + table[1 + q, k] for q in range(links)]
        others = jnp.concatenate([stack[index] for index in near], 1)
        kernel = jnp.exp2(tn(own_of(k), others))
        high = kernel.astype(BF16)
        highs[k] = high
        lows[k] = (kernel - high.astype(F32)).astype(BF16)
    sums = []
    for k in range(bins):
        heavy = [bins + k]
        for q in range(links):
            shift = table[1 + q, k]
            whole = d * bins + k + shift
            linked = (table[1 + links + q, k] != 0) & (whole >= 0) & (whole < n * bins)
            heavy.append(jnp.where(linked, bins + k + shift, 3 * bins))
        masses = jnp.concatenate([weighted[index] for index in heavy], 1)
        turned = jnp.transpose(nt(highs[k], masses) + nt(lows[k], masses))
        sums.append(turned[0:8] + turned[8:16])
    return sums


def contact_force(block, sums):
    gap = block * sums[3:4] - sums
    return stiffness * pltpu.roll(gap, 4, 0) - damping * gap


def flat_id():
    return (
        lax.axis_index("gx") * lax.axis_size("gy") + lax.axis_index("gy")
    ) * lax.axis_size("gz") + lax.axis_index("gz")


def first_body(
    n, links, own, before, after, *refs
):
    copies = fetch(refs[0:1], refs[9:10], refs[10])
    moved, moved_down, deposit, stack, weighted, highs, lows, norms, table = refs[1:10]
    bins = norms.shape[0]
    d = flat_id()
    row = iota((8, LANES), 0)
    lane = iota((8, LANES), 1)
    for k in range(bins, own.shape[0]):
        moved[k] = before[k]
        moved_down[k] = after[k]
    for k in range(bins):
        load_block(before[k], row, k, stack, weighted)
        norms[k : k + 1, :] = load_block(own[k], row, bins + k, stack, weighted)
        load_block(after[k], row, 2 * bins + k, stack, weighted)
    weighted[3 * bins] = jnp.zeros((16, LANES), BF16)
    for copy in copies:
        copy.wait()
    groups = LANES // n
    per_group = bins // groups
    field = jnp.where(row >= 4, row - 4, 3)
    sums = pair_sums(
        d,
        n,
        bins,
        links,
        lambda k: own_side(own[k], norms[k : k + 1, :], row),
        stack,
        weighted,
        highs,
        lows,
        table,
    )
    total = jnp.zeros((8, LANES), F32)
    for k in range(bins):
        block = own[k]
        force = contact_force(block, sums[k])
        occupied = jnp.where(lane < table[0, k], step_sub, 0.0)
        new_vel = block + occupied * (force - drag_rate * block)
        new_pos = block + occupied * pltpu.roll(new_vel, 4, 0)
        result = jnp.where(row < 3, new_pos, jnp.where(row == 3, block, new_vel))
        moved[k] = result
        moved_down[k] = result
        load = jnp.where(row == 3, block, block[3:4] * (block + new_vel))
        column = jnp.sum(load, axis=1, keepdims=True)
        base = slot_lane(0, k, n, bins)
        place = (lane == base + per_group * field) & (row >= 3) & (row < 7)
        total = total + jnp.where(place, column, 0.0)
    deposit[...] = jnp.broadcast_to(jnp.sum(total, axis=0, keepdims=True), (8, LANES))


def final_body(n, links, own, before, after, recv, scalars, part, around, planes, depth, *refs):
    outs, refs = refs[0:3], refs[3:]
    stack, weighted, highs, lows, norms, state, table, pos, vel, fluid = refs[0:10]
    copies = fetch([scalars], [table], refs[10])
    deposit(n, norms.shape[0], part, around, planes, depth, recv, fluid, *refs[12:15])
    written = fetch([fluid], outs[2:3], refs[11].at[2:3])
    bins = norms.shape[0]
    d = flat_id()
    row = iota((8, LANES), 0)
    lane = iota((8, LANES), 1)
    per_group = bins // (LANES // n)
    columns = [
        jnp.transpose(
            jnp.broadcast_to(jnp.sum(recv[:, part, :], axis=0, keepdims=True), (LANES, LANES))
        )
        for part in range(2)
    ]
    rate = jnp.where(row < 4, step_sub * step_sub, step_sub) * drag_rate

    def push(part, k):
        at = 4 * bins * part + 4 * k
        if part == 2:
            at = k // per_group * 8 * per_group + 4 * per_group + 4 * (k % per_group)
        pair = columns[part // 2][at // 8 * 8 : at // 8 * 8 + 8]
        other = pltpu.roll(pair, 4, 0)
        here = (row < 4) if at % 8 == 0 else (row >= 4)
        both = jnp.where(here, pair, other)
        return jnp.where((row == 3) | (row == 7), 0.0, both * rate), both

    for k in range(bins):
        load_block(before[k] + push(0, k)[0], row, k, stack, weighted)
        load_block(after[k] + push(2, k)[0], row, 2 * bins + k, stack, weighted)
    for copy in copies:
        copy.wait()
    for k in range(bins):
        block = own[k] + jnp.where(lane < table[0, k], push(1, k)[0], 0.0)
        state[k] = block
        norms[k : k + 1, :] = load_block(block, row, bins + k, stack, weighted)
    weighted[3 * bins] = jnp.zeros((16, LANES), BF16)
    sums = pair_sums(
        d,
        n,
        bins,
        links,
        lambda k: own_side(state[k], norms[k : k + 1, :], row),
        stack,
        weighted,
        highs,
        lows,
        table,
    )
    for k in range(bins):
        block = state[k]
        force = contact_force(block, sums[k])
        occupied = jnp.where(lane < table[0, k], step_sub, 0.0)
        fluid_seen = push(1, k)[1]
        new_vel = block + occupied * (force + drag_rate * (fluid_seen - block))
        new_pos = block + occupied * pltpu.roll(new_vel, 4, 0)
        for c in range(3):
            pos[c, k : k + 1, :] = new_pos[c : c + 1]
            vel[c, k : k + 1, :] = new_vel[c + 4 : c + 5]
    written += fetch([pos, vel], outs[0:2], refs[11])
    for copy in written:
        copy.wait()


def laplace(at, x):
    centre = at(x)
    tall, wide = centre.shape
    total = at(x + 1) + at(x - 1)
    total = total + pltpu.roll(centre, 1, 0) + pltpu.roll(centre, tall - 1, 0)
    total = total + pltpu.roll(centre, 1, 1) + pltpu.roll(centre, wide - 1, 1)
    return viscosity * (total - 6.0 * centre)


def stencil_body(
    n, bins, base, fluid, x_low, x_high, y_low, y_high, recv, around, part, planes, depth, faces, rates
):
    cx, cy, cz = fluid.shape[1:]
    tall, wide = 2 * cy, 2 * cz
    deep = cx + 4

    def chunk(dx, dy, dz):
        value = recv[jnp.clip(neighbour_id(dx, dy, dz), 0, n - 1)]
        return jnp.where(exists(dx, dy, dz), value, 0.0)

    def columns(dx, dy):
        above, below = chunk(dx, dy, 1), chunk(dx, dy, -1)
        faces[...] = jnp.zeros((LANES, LANES), F32)
        faces[0:2, :] = above[1:3]
        faces[cz - 2 : cz, :] = below[3:5]
        return jnp.transpose(faces[...])

    own_z = columns(0, 0)
    low_z, high_z = columns(-1, 0), columns(1, 0)
    left_z, right_z = columns(0, -1), columns(0, 1)
    x_on = [jnp.where(exists(-1, 0, 0), 1.0, 0.0), jnp.where(exists(1, 0, 0), 1.0, 0.0)]
    y_on = [jnp.where(exists(0, -1, 0), 1.0, 0.0), jnp.where(exists(0, 1, 0), 1.0, 0.0)]
    row = iota((cy, cz), 0)

    corners = {(dx, dy): chunk(dx, dy, 0) for dx in (-1, 1) for dy in (-1, 1)}

    def y_line(ref, j, c, x):
        at = (c * cx + x) * 2 + j
        return ref[base + at // 8, at % 8 : at % 8 + 1, :]

    for c in range(3):
        for x in range(-2, cx + 2):
            if x < 0:
                core = x_low[c, x + 2] * x_on[0]
            elif x >= cx:
                core = x_high[c, x - cx] * x_on[1]
            else:
                core = fluid[c, x]
            beyond = jnp.zeros((cy, cz), F32)
            if 0 <= x < cx:
                at = (c * cx + x) * cy
                beyond = own_z[at : at + cy]
            elif x == -1:
                at = (c * cx + cx - 1) * cy
                beyond = low_z[at : at + cy]
            elif x == cx:
                at = c * cx * cy
                beyond = high_z[at : at + cy]
            around[c, x % deep, 0:cy, 0:cz] = core
            around[c, x % deep, 0:cy, cz:wide] = beyond
            side = jnp.zeros((cy, cz), F32)
            side_z = jnp.zeros((cy, cz), F32)
            if 0 <= x < cx:
                side = jnp.where(row == 0, y_line(y_high, 0, c, x) * y_on[1], side)
                side = jnp.where(row == 1, y_line(y_high, 1, c, x) * y_on[1], side)
                side = jnp.where(row == cy - 2, y_line(y_low, 0, c, x) * y_on[0], side)
                side = jnp.where(row == cy - 1, y_line(y_low, 1, c, x) * y_on[0], side)
            elif x in (-1, cx):
                dx = -1 if x < 0 else 1
                side = jnp.where(row == 0, corners[dx, 1][5 + c : 6 + c], side)
                side = jnp.where(row == cy - 1, corners[dx, -1][5 + c : 6 + c], side)
            if 0 <= x < cx:
                at = (c * cx + x) * cy
                side_z = jnp.where(row == 0, right_z[at : at + 1], side_z)
                side_z = jnp.where(row == cy - 1, left_z[at + cy - 1 : at + cy], side_z)
            around[c, x % deep, cy:tall, 0:cz] = side
            around[c, x % deep, cy:tall, cz:wide] = side_z

    y_row, z_lane = iota((tall, wide), 0), iota((tall, wide), 1)
    inside = jnp.where(y_row < cy, 1.0, 0.0)
    inside = jnp.where(y_row == cy, y_on[1], jnp.where(y_row == tall - 1, y_on[0], inside))
    deep_on = jnp.where(z_lane < cz, 1.0, 0.0)
    deep_on = jnp.where(z_lane == cz, jnp.where(exists(0, 0, 1), 1.0, 0.0), deep_on)
    deep_on = jnp.where(z_lane == wide - 1, jnp.where(exists(0, 0, -1), 1.0, 0.0), deep_on)
    inside = inside * deep_on
    for c in range(3):
        for x in range(-1, cx + 1):
            rate = laplace(lambda i: around[c, i % deep], x) * inside
            if x < 0:
                rate = rate * x_on[0]
            elif x == cx:
                rate = rate * x_on[1]
            rates[c, x + 1] = rate
        for x in range(cx):
            again = laplace(lambda i: rates[c, i + 1], x)
            total = around[c, x] + rates[c, x + 1] + 0.5 * again
            part[c, x] = total[0:cy, 0:cz]
    locate(n, bins, (cx, cy, cz), recv, planes, depth)


def packed(n, ref, which):
    groups = LANES // n
    rows = [ref[:, which, :]]
    if n < LANES:
        rows.append(jnp.zeros((LANES - n, LANES), F32))
    turned = jnp.transpose(jnp.concatenate(rows, 0))
    span = LANES // groups
    total = turned[0:span]
    for g in range(1, groups):
        total = total + pltpu.roll(turned[g * span : (g + 1) * span], g * n, 1)
    return total


def locate(n, bins, sizes, ids, planes, depth):
    cx, cy, cz = sizes
    tall, wide = 2 * cy, 2 * cz
    per_group = bins // (LANES // n)
    where = packed(n, ids, 0)
    x = where[0:per_group] - (lax.axis_index("gx") * cx - 1).astype(F32)
    y = where[per_group : 2 * per_group] - (lax.axis_index("gy") * cy).astype(F32)
    z = where[2 * per_group : 3 * per_group] - (lax.axis_index("gz") * cz).astype(F32)
    near = (x >= 0) & (x < cx + 2) & (y >= -1) & (y <= cy) & (z >= -1) & (z <= cz)
    y = jnp.where(y < 0, y + tall, y)
    z = jnp.where(z < 0, z + wide, z)
    planes[...] = jnp.where(near, x * tall + y, -1.0)
    depth_code = jnp.where(near, z, -1.0).astype(jnp.int32)
    depth_row = iota((wide, LANES), 0)
    for r in range(per_group):
        depth[:, r * LANES : (r + 1) * LANES] = jnp.where(
            depth_code[r : r + 1] == depth_row, 1.0, 0.0
        ).astype(BF16)


def deposit(n, bins, part, around, planes, depth, recv, out, table, low_table, field):
    cx, cy, cz = part.shape[1:]
    deep = cx + 4
    tall = 2 * cy
    per_group = bins // (LANES // n)
    count = (cx + 2) * tall
    loads = packed(n, recv, 1)
    plane_code = planes[...].astype(jnp.int32)
    plane_row = iota((count, LANES), 0)
    for r in range(per_group):
        at = r * LANES
        hit = plane_code[r : r + 1] == plane_row
        for f in range(4):
            load = loads[f * per_group + r : f * per_group + r + 1]
            high, low = pieces_2(load)
            table[f * count : (f + 1) * count, at : at + LANES] = jnp.where(
                hit, high, 0.0
            ).astype(BF16)
            low_table[f * count : (f + 1) * count, at : at + LANES] = jnp.where(
                hit, low, 0.0
            ).astype(BF16)
    spread = nt(table[...], depth[...]) + nt(low_table[...], depth[...])
    factor = coupling * drag_rate * (2.0 - step_sub * drag_rate)
    for c in range(3):
        for i in range(cx + 2):
            moment = spread[c * count + i * tall : c * count + (i + 1) * tall]
            mass = spread[3 * count + i * tall : 3 * count + (i + 1) * tall]
            field[c, i] = (coupling * drag_rate) * moment - factor * around[
                c, (i - 1) % deep
            ] * mass
        for x in range(cx):
            rate = laplace(lambda i: field[c, i + 1], x)
            total = field[c, x + 1] + 0.5 * rate
            out[c, x] = part[c, x] + total[0:cy, 0:cz]


def ring(n, step):
    return [(i, (i + step) % n) for i in range(n)]


def step(positions, velocities, weights, counts, link_offset, link_mask, bin_box, bin_cell, fluid):
    n = lax.axis_size(AXES)
    nx, ny = lax.axis_size("gx"), lax.axis_size("gy")
    bins = positions.shape[1]
    cx, cy, cz = fluid.shape[1:]
    offset, mask = link_offset.T, link_mask.T
    face_blocks = -(-6 * cx // 8)
    relay = lax.axis_size("gz") == 2

    links = offset.shape[0]
    up, down, send, face_low, face_high, table = call(
        functools.partial(prep_body, n),
        [(bins + face_blocks, 8, LANES)] * 2
        + [(n, 8, LANES)]
        + [(3, 2, cy, cz)] * 2
        + [((8, LANES), jnp.int32)],
        [HBM] * 10,
        [
            pltpu.VMEM(positions.shape, F32),
            pltpu.VMEM(velocities.shape, F32),
            pltpu.VMEM(weights.shape, F32),
            pltpu.VMEM(fluid.shape, F32),
            pltpu.SMEM((bins,), jnp.int32),
            pltpu.SMEM((bins,), jnp.int32),
            pltpu.SMEM((bins,), jnp.int32),
            pltpu.VMEM((1, bins), jnp.int32),
            pltpu.VMEM(offset.shape, jnp.int32),
            pltpu.VMEM(mask.shape, jnp.int32),
            pltpu.SemaphoreType.DMA((10,)),
            pltpu.VMEM((n, 8, LANES), F32),
            pltpu.SemaphoreType.DMA((1,)),
        ],
        [VMEM] * 2 + [HBM] + [VMEM] * 3,
    )(
        *[
            pltpu.with_memory_space_constraint(value, pltpu.HBM)
            for value in (
                positions,
                velocities,
                weights,
                fluid,
                counts,
                bin_box[:, 0],
                bin_cell,
                counts[None],
                offset,
                mask,
            )
        ]
    )
    ids = lax.all_to_all(send, AXES, 0, 0, tiled=True)
    before = lax.ppermute(up, AXES, ring(n, 1))
    after = lax.ppermute(down, AXES, ring(n, -1))
    x_low = lax.ppermute(face_high, "gx", ring(nx, 1))
    x_high = lax.ppermute(face_low, "gx", ring(nx, -1))

    pair_scratch = [
        pltpu.VMEM((3 * bins + 1, 48, LANES), BF16),
        pltpu.VMEM((3 * bins + 1, 16, LANES), BF16),
        pltpu.VMEM((bins, LANES, (offset.shape[0] + 1) * LANES), BF16),
        pltpu.VMEM((bins, LANES, (offset.shape[0] + 1) * LANES), BF16),
    ]
    held = [pltpu.SMEM((8, LANES), jnp.int32)]
    moved, moved_down, deposits = call(
        functools.partial(first_body, n, links),
        [(bins + face_blocks, 8, LANES)] * 2 + [(8, LANES)],
        [VMEM] * 4,
        pair_scratch
        + [pltpu.VMEM((bins, LANES), F32)]
        + held
        + [pltpu.SemaphoreType.DMA((1,))],
    )(up, before, after, table)
    (send,) = call(functools.partial(gather_body, n, bins), [(n, 2, LANES)], [VMEM] * 3)(
        ids, fluid, deposits
    )
    replies = lax.all_to_all(send, AXES, 0, 0, tiled=True)
    before = lax.ppermute(moved, AXES, ring(n, 1))
    after = lax.ppermute(moved_down, AXES, ring(n, -1))

    y_low, y_high, base = before, after, bins
    if not relay:
        y_low = lax.ppermute(up[bins:], "gy", ring(ny, 1))
        y_high = lax.ppermute(down[bins:], "gy", ring(ny, -1))
        base = 0
    lanes = bins * n
    per_group = bins // (LANES // n)
    around, part, planes, depth = call(
        functools.partial(stencil_body, n, bins, base),
        [(3, cx + 4, 2 * cy, 2 * cz), (3, cx, cy, cz), (per_group, LANES), ((2 * cz, lanes), BF16)],
        [VMEM] * 6,
        [pltpu.VMEM((LANES, LANES), F32), pltpu.VMEM((3, cx + 2, 2 * cy, 2 * cz), F32)],
    )(fluid, x_low, x_high, y_low, y_high, ids)
    count = (cx + 2) * 2 * cy
    positions_out, velocities_out, fluid_out = call(
        functools.partial(final_body, n, links),
        [positions.shape, velocities.shape, fluid.shape],
        [VMEM] * 9,
        pair_scratch
        + [pltpu.VMEM((bins, LANES), F32), pltpu.VMEM((bins, 8, LANES), F32)]
        + held
        + [
            pltpu.VMEM(positions.shape, F32),
            pltpu.VMEM(velocities.shape, F32),
            pltpu.VMEM(fluid.shape, F32),
            pltpu.SemaphoreType.DMA((1,)),
            pltpu.SemaphoreType.DMA((3,)),
            pltpu.VMEM((4 * count, lanes), BF16),
            pltpu.VMEM((4 * count, lanes), BF16),
            pltpu.VMEM((3, cx + 2, 2 * cy, 2 * cz), F32),
        ],
        [HBM] * 3,
    )(moved, before, after, replies, table, part, around, planes, depth)
    return positions_out, velocities_out, fluid_out


def solution(mesh):
    in_specs = (
        P(None, AXES, None),
        P(None, AXES, None),
        P(AXES, None),
        P(AXES),
        P(AXES, None),
        P(AXES, None),
        P(AXES, None),
        P(AXES),
        P(None, "gx", "gy", "gz"),
    )
    out_specs = (
        P(None, AXES, None),
        P(None, AXES, None),
        P(None, "gx", "gy", "gz"),
    )
    return jax.shard_map(step, mesh=mesh, in_specs=in_specs, out_specs=out_specs, check_vma=False)
```
